512 devices in a mesh: grid: 16 (over y, core), tile: 32 (over x, z).
Axes of the slice: x: 4, y: 8, z: 8, core: 2. Of those that a mesh axis runs over, the one named last changes fastest.
Arguments:
- rhs_local: bfloat16 [192, 786432], P(None, ('grid', 'tile')), may hold values from -6 to 6
- diag_inv: bfloat16 [1536, 512, 512], P(('grid', 'tile')), may hold values from -1 to 2, as said below
- codes: bfloat16 [327680, 1536], P(('grid', 'tile')), may hold values from -127 to 127, as said below
- row_scales: float32 [327680], P(('grid', 'tile')), may hold values from 0 to 1, as said below
- sep_index: int32 [327680], P(('grid', 'tile')), may hold values from 0 to 2559, as said below
- live_rows: int32 [512], P(('grid', 'tile')), may hold values from 160 to 640, as said below
- rhs_sep: bfloat16 [192, 2560], P(None, 'tile'), may hold values from -6 to 6
- root_inv: bfloat16 [2560, 2560], P('tile'), may hold values from -1 to 2, as said below
Outputs:
- solution_local: bfloat16 [192, 786432], P(None, ('grid', 'tile'))
- solution_sep: float32 [192, 2560], P(None, 'tile')
The draws below stay inside these ranges and needn't reach their ends.
Inputs may be any that keep to these rules, and one draw needn't show every extreme that they name: `diag_inv`: each block is upper triangular. `root_inv`: each block is upper triangular. `codes`: Integers. `row_scales`: Positive. `sep_index`: of each device's 640 entries, the j-th run of 20 consecutive entries lies in j * 80 to (j + 1) * 80 - 1, and the entries of one run are distinct. `live_rows`: some device has all 640 rows live.
All inputs are finite; a program needn't handle non-finite values.
Results may differ from the reference program's by a relative error of at most 0.0054.
Values may be sent and summed in bfloat16 or wider, within the bound.
No kernel may reach another device: no remote copies, remote signals or barrier semaphores. Data moves between devices by JAX's collectives and lax.ppermute only.
A program may use at most 64 MiB of HBM per device.

```python
import math
import jax
import jax.numpy as jnp
from jax import lax

RHS = 192
BLOCK = 512
PER_DEV = 3
CROWS = 640
SEP = 2560
LOCAL = 1536
MEMBERS = 512
BLOCKS = 1536
COUPLED = 327680
UNKNOWNS = 786432
N_TILE = 32


def upper_blocks(key, count, order):
    keys = jax.random.split(key, 2)
    diagonal = jax.random.uniform(keys[0], (count, order), jnp.float32, 0.7, 1.3)
    upper = jax.random.normal(keys[1], (count, order, order), jnp.float32) * (0.6 / math.sqrt(order))
    upper = jnp.clip(upper, -0.9, 0.9)
    strict = jnp.triu(jnp.ones((order, order), jnp.float32), 1)
    eye = jnp.eye(order, dtype=jnp.float32)
    return upper * strict[None] + diagonal[:, :, None] * eye[None]


def draw_diag_inv(key, part):
    return upper_blocks(key, BLOCKS, BLOCK).astype(jnp.bfloat16)


def draw_root_inv(key, part):
    return upper_blocks(key, 1, SEP)[0].astype(jnp.bfloat16)


def draw_codes(key, part):
    values = jax.random.randint(key, (COUPLED, LOCAL), -127, 128)
    return values.astype(jnp.float32).astype(jnp.bfloat16)


def draw_row_scales(key, part):
    spread = jax.random.uniform(key, (COUPLED,), jnp.float32, math.log(0.2), math.log(2.0))
    norming = 73.0 * math.sqrt(LOCAL * COUPLED / SEP)
    return (jnp.exp(spread) / norming).astype(jnp.float32)


def draw_sep_index(key, part):
    share_len = SEP // N_TILE
    per_share = CROWS // N_TILE
    keys = jax.random.split(key, MEMBERS * N_TILE)
    picks = jax.vmap(lambda member_key: jax.random.permutation(member_key, share_len)[:per_share])(keys)
    picks = picks.reshape(MEMBERS, N_TILE, per_share).astype(jnp.int32)
    starts = (jnp.arange(N_TILE, dtype=jnp.int32) * share_len)[None, :, None]
    return (picks + starts).reshape(COUPLED).astype(jnp.int32)


def draw_live_rows(key, part):
    keys = jax.random.split(key, 2)
    counts = jax.random.randint(keys[0], (MEMBERS,), max(1, CROWS // 4), CROWS + 1)
    chosen = jax.random.randint(keys[1], (), 0, MEMBERS)
    return counts.at[chosen].set(CROWS).astype(jnp.int32)


def steps_of(stream_key, extent, cuts, smallest, high):
    def one(dim, blocks):
        draws = jax.random.uniform(jax.random.fold_in(jax.random.fold_in(stream_key, 6), dim), (blocks,), jnp.float32, smallest / len(cuts), high / len(cuts))
        return jnp.repeat(jnp.exp(draws), extent[dim] // blocks).reshape((-1,) + (1,) * (len(extent) - dim - 1))

    level = one(*cuts[0])
    for cut in cuts[1:]:
        level = level * one(*cut)
    return level


def gaussian(stream_key, extent, deviation, bound, pieces=(), kind=jnp.bfloat16):
    drawn = jax.random.normal(stream_key, extent, jnp.float32) * deviation
    if len(pieces) > 0:
        drawn = steps_of(stream_key, extent, pieces, -0.22, 0.18) * drawn
    return jnp.clip(drawn, min=-bound, max=bound).astype(kind)


def setup_inputs(seed: int = 0) -> dict:
    seeds = jax.random.split(jax.random.key(seed), 9)
    return {
        "rhs_local": gaussian(seeds[0], (RHS, UNKNOWNS), 1.0, 6.0, ((1, 512),)),
        "diag_inv": draw_diag_inv(jax.random.fold_in(seeds[8], 71), 0),
        "codes": draw_codes(jax.random.fold_in(seeds[8], 71), 0),
        "row_scales": draw_row_scales(jax.random.fold_in(seeds[8], 71), 0),
        "sep_index": draw_sep_index(jax.random.fold_in(seeds[8], 71), 0),
        "live_rows": draw_live_rows(jax.random.fold_in(seeds[8], 71), 0),
        "rhs_sep": gaussian(seeds[6], (RHS, SEP), 1.0, 6.0, ((1, 32),)),
        "root_inv": draw_root_inv(jax.random.fold_in(seeds[8], 71), 0),
    }


def product(left, right):
    return jnp.dot(left.astype(jnp.float32), right.astype(jnp.float32), precision=lax.Precision.HIGHEST)


def reference(rhs_local, diag_inv, codes, row_scales, sep_index, live_rows, rhs_sep, root_inv):
    rhs_parts = rhs_local.reshape(RHS, MEMBERS, PER_DEV, BLOCK).transpose(1, 0, 2, 3)
    inv_parts = diag_inv.reshape(MEMBERS, PER_DEV, BLOCK, BLOCK)
    code_parts = codes.reshape(MEMBERS, CROWS, LOCAL)
    scale_parts = row_scales.reshape(MEMBERS, CROWS)
    index_parts = sep_index.reshape(MEMBERS, CROWS)
    positions = jnp.arange(CROWS, dtype=jnp.int32)
    factors = scale_parts * (positions[None, :] < live_rows[:, None]).astype(jnp.float32)

    def forward_step(summed, items):
        blocked, inverse, coded, row_factor, indices = items
        forward = jnp.einsum('rkb,kbc->rkc', blocked.astype(jnp.float32), inverse.astype(jnp.float32),
                             precision=lax.Precision.HIGHEST).astype(jnp.bfloat16).reshape(RHS, LOCAL)
        coupled = product(forward, coded.T) * row_factor[None, :]
        summed = summed.at[:, indices].add(coupled)
        return summed, forward

    summed, forwards = lax.scan(forward_step, jnp.zeros((RHS, SEP), jnp.float32),
                                (rhs_parts, inv_parts, code_parts, factors, index_parts))
    residue = (rhs_sep.astype(jnp.float32) - summed).astype(jnp.bfloat16)
    forward_sep = product(residue, root_inv).astype(jnp.bfloat16)
    solution_sep = product(forward_sep, root_inv.T)
    rounded_sep = solution_sep.astype(jnp.bfloat16)

    def backward_step(items):
        forward, inverse, coded, row_factor, indices = items
        picked = rounded_sep[:, indices]
        weighted = (picked.astype(jnp.float32) * row_factor[None, :]).astype(jnp.bfloat16)
        update = product(weighted, coded)
        misfit = (forward.astype(jnp.float32) - update).astype(jnp.bfloat16).reshape(RHS, PER_DEV, BLOCK)
        result = jnp.einsum('rkc,kbc->rkb', misfit.astype(jnp.float32), inverse.astype(jnp.float32),
                            precision=lax.Precision.HIGHEST).astype(jnp.bfloat16)
        return result.reshape(RHS, LOCAL)

    results = lax.map(backward_step, (forwards, inv_parts, code_parts, factors, index_parts))
    solution_local = results.transpose(1, 0, 2).reshape(RHS, UNKNOWNS)
    return solution_local, solution_sep
```

```python
import jax
import jax.numpy as jnp
from jax import lax
from jax.sharding import PartitionSpec as P

LANES = 128


def round_up(value, step):
    return -(-value // step) * step


def on_device(rhs_local, diag_inv, codes, row_scales, sep_index, live_rows, rhs_sep, root_inv):
    rhs_count, local_len = rhs_local.shape
    per_dev, block_len = (diag_inv.shape[0], diag_inv.shape[1])
    coupled_rows = codes.shape[0]
    share_len, sep_len = root_inv.shape
    tile_count = lax.axis_size("tile")
    grid_count = lax.axis_size("grid")
    per_share = coupled_rows // tile_count
    chunk_rows = round_up(per_share, 8)
    own_rhs = rhs_count // grid_count
    value_lanes = round_up(rhs_count + 1, LANES)
    share_lanes = round_up(share_len, LANES)

    pieces = []
    for block_pos in range(per_dev):
        columns = rhs_local[:, block_pos * block_len : (block_pos + 1) * block_len]
        pieces.append(jnp.dot(columns, diag_inv[block_pos], preferred_element_type=jnp.float32))
    forward_flat = jnp.concatenate(pieces, axis=1).astype(jnp.bfloat16)
    positions = jnp.arange(coupled_rows, dtype=jnp.int32)
    row_factor = row_scales * (positions < live_rows[0]).astype(jnp.float32)
    coupled = (
        lax.dot_general(
            codes, forward_flat, (((1,), (1,)), ((), ())), preferred_element_type=jnp.float32
        )
        * row_factor[:, None]
    )
    offsets = (sep_index - positions // per_share * share_len).astype(jnp.float32)
    payload = jnp.concatenate(
        [
            coupled,
            offsets[:, None],
            jnp.zeros((coupled_rows, value_lanes - rhs_count - 1), jnp.float32),
        ],
        axis=1,
    )
    payload = payload.reshape(tile_count, per_share, value_lanes)
    payload = jnp.pad(payload, ((0, 0), (0, chunk_rows - per_share), (0, 0))).astype(jnp.bfloat16)
    arrived = lax.all_to_all(payload, "tile", 0, 0, tiled=True)
    arrived = arrived.reshape(tile_count * chunk_rows, value_lanes)
    columns = jnp.arange(share_lanes, dtype=jnp.int32).astype(jnp.bfloat16)
    onehot = (arrived[:, rhs_count : rhs_count + 1] == columns[None, :]).astype(jnp.bfloat16)
    partial_value = lax.dot_general(
        arrived[:, :rhs_count],
        onehot,
        (((0,), (0,)), ((), ())),
        preferred_element_type=jnp.float32,
    )
    partial_value = partial_value.reshape(grid_count, own_rhs, share_lanes)
    own_share = lax.all_to_all(partial_value, "grid", 0, 0, tiled=True).sum(axis=0)
    own_right = lax.dynamic_slice_in_dim(rhs_sep, lax.axis_index("grid") * own_rhs, own_rhs, 0)
    residue = (own_right.astype(jnp.float32) - own_share[:, :share_len]).astype(jnp.bfloat16)
    spaced = root_inv.reshape(share_len, tile_count, share_len)
    spaced = jnp.pad(spaced, ((0, 0), (0, 0), (0, share_lanes - share_len)))
    spaced = spaced.reshape(share_len, tile_count * share_lanes)
    root_part = jnp.dot(residue, spaced, preferred_element_type=jnp.float32)
    root_part = root_part.reshape(own_rhs, tile_count, share_lanes).transpose(1, 0, 2)
    forward_sep = lax.all_to_all(root_part, "tile", 0, 0, tiled=True).sum(axis=0)
    forward_sep = jnp.broadcast_to(
        forward_sep.astype(jnp.bfloat16)[None], (tile_count, own_rhs, share_lanes)
    )
    forward_sep = lax.all_to_all(forward_sep, "tile", 0, 0, tiled=True)
    forward_sep = forward_sep.transpose(1, 0, 2).reshape(own_rhs, tile_count * share_lanes)
    solved = lax.dot_general(
        forward_sep, spaced, (((1,), (1,)), ((), ())), preferred_element_type=jnp.float32
    )
    solved = jnp.broadcast_to(solved[None], (grid_count, own_rhs, share_len))
    solved = lax.all_to_all(solved, "grid", 0, 0, tiled=True).reshape(rhs_count, share_len)
    picked = lax.dot_general(
        onehot[:, :share_len],
        solved.astype(jnp.bfloat16),
        (((1,), (1,)), ((), ())),
        preferred_element_type=jnp.float32,
    ).astype(jnp.bfloat16)
    picked = picked.reshape(tile_count, chunk_rows, rhs_count)
    picked = lax.all_to_all(picked, "tile", 0, 0, tiled=True)
    picked = picked[:, :per_share].reshape(coupled_rows, rhs_count)
    weighted = (picked.astype(jnp.float32) * row_factor[:, None]).astype(jnp.bfloat16)
    update = lax.dot_general(
        weighted, codes, (((0,), (0,)), ((), ())), preferred_element_type=jnp.float32
    )
    misfit = (forward_flat.astype(jnp.float32) - update).astype(jnp.bfloat16)
    results = []
    for block_pos in range(per_dev):
        columns = misfit[:, block_pos * block_len : (block_pos + 1) * block_len]
        results.append(
            lax.dot_general(
                columns,
                diag_inv[block_pos],
                (((1,), (1,)), ((), ())),
                preferred_element_type=jnp.float32,
            )
        )
    result = jnp.concatenate(results, axis=1)
    return (result.astype(jnp.bfloat16), solved)


def solution(mesh):
    return jax.shard_map(
        on_device,
        mesh=mesh,
        in_specs=(
            P(None, ("grid", "tile")),
            P(("grid", "tile"), None, None),
            P(("grid", "tile"), None),
            P(("grid", "tile")),
            P(("grid", "tile")),
            P(("grid", "tile")),
            P(None, "tile"),
            P("tile", None),
        ),
        out_specs=(P(None, ("grid", "tile")), P(None, "tile")),
        check_vma=False,
    )
```

```python
import functools

import jax
import jax.numpy as jnp
from jax import lax
from jax.experimental import pallas as pl
from jax.experimental.pallas import tpu as pltpu
from jax.sharding import PartitionSpec as P

LANES = 128
HALF = 64
F32 = jnp.float32
BF16 = jnp.bfloat16
VMEM_BYTES = 24 * 1024 * 1024
ANY = pl.BlockSpec(memory_space=pl.ANY)
VMEM = pl.BlockSpec(memory_space=pltpu.VMEM)
SMEM = pl.BlockSpec(memory_space=pltpu.SMEM)


def round_up(value, step):
    return -(-value // step) * step


def factor_columns(scales_ref, live_ref):
    groups = scales_ref.shape[0]
    row = lax.broadcasted_iota(jnp.int32, (groups, LANES), 0)
    lane = lax.broadcasted_iota(jnp.int32, (groups, LANES), 1)
    live = (row * LANES + lane) < live_ref[0]
    factors = scales_ref[...] * live.astype(F32)
    if groups < LANES:
        factors = jnp.concatenate([factors, jnp.zeros((LANES - groups, LANES), F32)], axis=0)
    return factors.T


def dot(left, right, left_dim=1, right_dim=0):
    return lax.dot_general(
        left, right, (((left_dim,), (right_dim,)), ((), ())), preferred_element_type=F32
    )


def forward_kernel(
    per_share, rhs_hbm, diag_hbm, codes_hbm, scales_ref, offsets_ref, live_ref,
    forward_ref, chunks_ref,
    rhs, diag, codes, coupled, packed, sems,
):
    blocks, block_len = diag.shape[0], diag.shape[1]
    rows, rhs_count = codes.shape[0], rhs.shape[0]
    half = per_share // 2
    copies = [pltpu.make_async_copy(rhs_hbm, rhs, sems.at[0])]
    for block in range(blocks):
        copies.append(
            pltpu.make_async_copy(diag_hbm.at[block], diag.at[block], sems.at[1 + block])
        )
    copies.append(pltpu.make_async_copy(codes_hbm, codes, sems.at[1 + blocks]))
    for copy in copies:
        copy.start()
    factors = factor_columns(scales_ref, live_ref)
    packed[...] = jnp.zeros_like(packed)
    copies[0].wait()
    for block in range(blocks):
        copies[1 + block].wait()
        columns = slice(block * block_len, (block + 1) * block_len)
        forward_ref[:, columns] = dot(rhs[:, columns], diag[block]).astype(BF16)
    copies[-1].wait()
    for group in range(0, rows, LANES):
        span = slice(group, min(group + LANES, rows))
        count = span.stop - span.start
        value = dot(codes[span, :], forward_ref[...], 1, 1)
        value = value * factors[:count, group // LANES : group // LANES + 1]
        coupled[span, :LANES] = value[:, :LANES]
        tail = value[:, LANES:]
        coupled[span, LANES : LANES + HALF] = tail
        coupled[span, LANES + HALF :] = tail
    low_lane = lax.broadcasted_iota(jnp.int32, (half, LANES), 1) < HALF
    for peer in range(rows // per_share):
        first = peer * per_share
        packed[peer, :per_share, :] = coupled[first : first + per_share, :LANES]
        packed[peer, per_share : per_share + half, :] = jnp.where(
            low_lane,
            coupled[first : first + half, LANES:],
            coupled[first + half : first + per_share, LANES:],
        )
        packed[peer, per_share + half : per_share + half + 1, :] = offsets_ref[peer : peer + 1, :]
    chunks_ref[...] = packed[...].astype(BF16)


def sum_kernel(per_share, chunks_ref, hot_ref, sums_ref, wide, table, total):
    peers, chunk_rows = chunks_ref.shape[0], chunks_ref.shape[1]
    members, own_pad = sums_ref.shape[0], sums_ref.shape[1]
    half = per_share // 2
    wide[...] = chunks_ref[...].astype(F32)
    for peer in range(peers):
        table[peer : peer + 1, :] = wide[peer, per_share + half : per_share + half + 1, :]
    if peers < LANES:
        table[peers:, :] = jnp.zeros((LANES - peers, LANES), F32)
    offsets = table[...].T
    row = lax.broadcasted_iota(jnp.int32, (LANES, LANES), 0)
    tail_row = jnp.logical_and(row >= per_share, row < per_share + half)
    shifts = (
        jnp.where(row < per_share, offsets, -1.0),
        jnp.where(tail_row, pltpu.roll(offsets, per_share, 0), -1.0),
        jnp.where(tail_row, pltpu.roll(offsets, half, 0), -1.0),
    )
    lane = lax.broadcasted_iota(jnp.int32, (chunk_rows, LANES), 1).astype(F32)
    for peer in range(peers):
        span = slice(peer * chunk_rows, (peer + 1) * chunk_rows)
        for part, shifted in enumerate(shifts):
            hit = shifted[:chunk_rows, peer : peer + 1] == lane
            hot_ref[span, part * LANES : (part + 1) * LANES] = hit.astype(F32).astype(BF16)
    values = wide[...].reshape(peers * chunk_rows, LANES).T.astype(BF16)
    result = dot(values, hot_ref[...])
    total[:LANES, :] = result[:, :LANES]
    total[LANES:, :] = result[:HALF, LANES : 2 * LANES] + result[HALF:, 2 * LANES :]
    own = total.shape[0] // members
    if own < own_pad:
        sums_ref[...] = jnp.zeros_like(sums_ref)
    for member in range(members):
        sums_ref[member, :own, :] = total[member * own : (member + 1) * own, :].astype(BF16)


def spread_kernel(own, solved_ref, solution_ref, picker_ref, wide, total):
    members = solved_ref.shape[0]
    wide[...] = solved_ref[...].astype(F32)
    for member in range(members):
        total[member * own : (member + 1) * own, :] = wide[member, :own, :]
    value = total[...]
    tail = value[LANES:, :].astype(BF16)
    nothing = jnp.zeros((HALF, LANES), BF16)
    picker_ref[:, :LANES] = value[:LANES, :].astype(BF16)
    picker_ref[:HALF, LANES : 2 * LANES] = tail
    picker_ref[HALF:, LANES : 2 * LANES] = nothing
    picker_ref[:HALF, 2 * LANES :] = nothing
    picker_ref[HALF:, 2 * LANES :] = tail
    padded = jnp.concatenate([value, jnp.zeros((HALF, LANES), F32)], axis=0)
    flipped = padded.T
    solution_ref[...] = flipped[: solution_ref.shape[0], : solution_ref.shape[1]]


def backward_kernel(
    per_share, chunks_ref, scales_ref, live_ref, forward_ref, codes_hbm, diag_hbm,
    result_ref,
    codes, diag, wide, picked, sems,
):
    blocks, block_len = diag.shape[0], diag.shape[1]
    rows, rhs_count = codes.shape[0], forward_ref.shape[0]
    half = per_share // 2
    copies = [pltpu.make_async_copy(codes_hbm, codes, sems.at[0])]
    for block in range(blocks):
        copies.append(
            pltpu.make_async_copy(diag_hbm.at[block], diag.at[block], sems.at[1 + block])
        )
    for copy in copies:
        copy.start()
    factors = factor_columns(scales_ref, live_ref)
    wide[...] = chunks_ref[...].astype(F32)
    for peer in range(rows // per_share):
        first = peer * per_share
        picked[first : first + per_share, :LANES] = wide[peer, :per_share, :]
        tail = wide[peer, per_share : per_share + half, :]
        picked[first : first + half, LANES:] = tail
        picked[first + half : first + per_share, LANES:] = pltpu.roll(tail, HALF, 1)
    weighted = []
    for group in range(0, rows, LANES):
        span = slice(group, min(group + LANES, rows))
        count = span.stop - span.start
        value = picked[span, :] * factors[:count, group // LANES : group // LANES + 1]
        weighted.append(value.T[:rhs_count].astype(BF16))
    weighted = jnp.concatenate(weighted, axis=1)
    copies[0].wait()
    for block in range(blocks):
        columns = slice(block * block_len, (block + 1) * block_len)
        update = dot(weighted, codes[:, columns])
        misfit = (forward_ref[:, columns].astype(F32) - update).astype(BF16)
        copies[1 + block].wait()
        result_ref[:, columns] = dot(misfit, diag[block], 1, 1).astype(BF16)


def params():
    return pltpu.CompilerParams(vmem_limit_bytes=VMEM_BYTES)


def cost(flops, moved):
    return pl.CostEstimate(flops=flops, bytes_accessed=moved, transcendentals=0)


def on_device(rhs_local, diag_inv, codes, row_scales, sep_index, live_rows, rhs_sep, root_inv):
    rhs_count, local_len = rhs_local.shape
    per_dev, block_len = (diag_inv.shape[0], diag_inv.shape[1])
    coupled_rows = codes.shape[0]
    share_len, sep_len = root_inv.shape
    tile_count = lax.axis_size("tile")
    grid_count = lax.axis_size("grid")
    per_share = coupled_rows // tile_count
    chunk_rows = round_up(per_share + per_share // 2 + 1, 16)
    own_rhs = rhs_count // grid_count
    own_pad = round_up(own_rhs, 16)

    groups = -(-coupled_rows // LANES)
    scales = jnp.pad(row_scales, (0, groups * LANES - coupled_rows)).reshape(groups, LANES)
    starts = jnp.arange(tile_count, dtype=jnp.int32)[:, None] * share_len
    offsets = (sep_index.reshape(tile_count, per_share) - starts).astype(F32)
    offsets = jnp.pad(offsets, ((0, 0), (0, LANES - per_share)))

    forward_flat, chunks = pl.pallas_call(
        functools.partial(forward_kernel, per_share),
        out_shape=(
            jax.ShapeDtypeStruct((rhs_count, local_len), BF16),
            jax.ShapeDtypeStruct((tile_count, chunk_rows, LANES), BF16),
        ),
        in_specs=[ANY, ANY, ANY, VMEM, VMEM, SMEM],
        out_specs=(VMEM, VMEM),
        scratch_shapes=[
            pltpu.VMEM((rhs_count, local_len), BF16),
            pltpu.VMEM(diag_inv.shape, BF16),
            pltpu.VMEM(codes.shape, BF16),
            pltpu.VMEM((coupled_rows, 2 * LANES), F32),
            pltpu.VMEM((tile_count, chunk_rows, LANES), F32),
            pltpu.SemaphoreType.DMA((2 + per_dev,)),
        ],
        compiler_params=params(),
        cost_estimate=cost(2 * rhs_count * local_len * (block_len + coupled_rows), 5 << 20),
        name="forward",
    )(rhs_local, diag_inv, codes, scales, offsets, live_rows)
    arrived = lax.all_to_all(chunks, "tile", 0, 0, tiled=True)
    onehot, sums = pl.pallas_call(
        functools.partial(sum_kernel, per_share),
        out_shape=(
            jax.ShapeDtypeStruct((tile_count * chunk_rows, 3 * LANES), BF16),
            jax.ShapeDtypeStruct((grid_count, own_pad, LANES), BF16),
        ),
        in_specs=[VMEM],
        out_specs=(VMEM, VMEM),
        scratch_shapes=[
            pltpu.VMEM((tile_count, chunk_rows, LANES), F32),
            pltpu.VMEM((LANES, LANES), F32),
            pltpu.VMEM((rhs_count, LANES), F32),
        ],
        compiler_params=params(),
        cost_estimate=cost(2 * tile_count * chunk_rows * 3 * LANES * LANES, 1 << 20),
        name="gather_sum",
    )(arrived)
    own_share = lax.all_to_all(sums, "grid", 0, 0, tiled=True).astype(F32).sum(axis=0)
    own_right = lax.dynamic_slice_in_dim(rhs_sep, lax.axis_index("grid") * own_rhs, own_rhs, 0)
    own_right = jnp.pad(own_right, ((0, own_pad - own_rhs), (0, LANES - share_len)))
    residue = (own_right.astype(F32) - own_share)[:, :share_len].astype(BF16)
    spaced = root_inv.reshape(share_len, tile_count, share_len)
    spaced = jnp.pad(spaced, ((0, 0), (0, 0), (0, LANES - share_len)))
    spaced = spaced.reshape(share_len, tile_count * LANES)
    root_part = jnp.dot(residue, spaced, preferred_element_type=F32).astype(BF16)
    root_part = root_part.reshape(own_pad, tile_count, LANES).transpose(1, 0, 2)
    forward_sep = lax.all_to_all(root_part, "tile", 0, 0, tiled=True).astype(F32).sum(axis=0)
    forward_sep = jnp.broadcast_to(
        forward_sep.astype(BF16)[None], (tile_count, own_pad, LANES)
    )
    forward_sep = lax.all_to_all(forward_sep, "tile", 0, 0, tiled=True)
    forward_sep = forward_sep.transpose(1, 0, 2).reshape(own_pad, tile_count * LANES)
    solved = dot(forward_sep, spaced, 1, 1)
    solved = jnp.pad(solved.astype(BF16), ((0, 0), (0, LANES - share_len)))
    solved = jnp.broadcast_to(solved[None], (grid_count, own_pad, LANES))
    solved = lax.all_to_all(solved, "grid", 0, 0, tiled=True)
    solution_sep, picker = pl.pallas_call(
        functools.partial(spread_kernel, own_rhs),
        out_shape=(
            jax.ShapeDtypeStruct((share_len, rhs_count), F32),
            jax.ShapeDtypeStruct((LANES, 3 * LANES), BF16),
        ),
        in_specs=[VMEM],
        out_specs=(VMEM, VMEM),
        scratch_shapes=[
            pltpu.VMEM((grid_count, own_pad, LANES), F32),
            pltpu.VMEM((rhs_count, LANES), F32),
        ],
        compiler_params=params(),
        name="spread",
    )(solved)
    picked = dot(onehot, picker, 1, 1).astype(BF16)
    picked = picked.reshape(tile_count, chunk_rows, LANES)
    picked = lax.all_to_all(picked, "tile", 0, 0, tiled=True)
    result = pl.pallas_call(
        functools.partial(backward_kernel, per_share),
        out_shape=jax.ShapeDtypeStruct((rhs_count, local_len), BF16),
        in_specs=[VMEM, VMEM, SMEM, VMEM, ANY, ANY],
        out_specs=VMEM,
        scratch_shapes=[
            pltpu.VMEM(codes.shape, BF16),
            pltpu.VMEM(diag_inv.shape, BF16),
            pltpu.VMEM((tile_count, chunk_rows, LANES), F32),
            pltpu.VMEM((coupled_rows, 2 * LANES), F32),
            pltpu.SemaphoreType.DMA((1 + per_dev,)),
        ],
        compiler_params=params(),
        cost_estimate=cost(2 * rhs_count * local_len * (block_len + coupled_rows), 5 << 20),
        name="backward",
    )(picked, scales, live_rows, forward_flat, codes, diag_inv)
    return (result, solution_sep.T)


def solution(mesh):
    return jax.shard_map(
        on_device,
        mesh=mesh,
        in_specs=(
            P(None, ("grid", "tile")),
            P(("grid", "tile"), None, None),
            P(("grid", "tile"), None),
            P(("grid", "tile")),
            P(("grid", "tile")),
            P(("grid", "tile")),
            P(None, "tile"),
            P("tile", None),
        ),
        out_specs=(P(None, ("grid", "tile")), P(None, "tile")),
        check_vma=False,
    )
```

```python
import functools

import jax
import jax.numpy as jnp
from jax import lax
from jax.experimental import pallas as pl
from jax.experimental.pallas import tpu as pltpu
from jax.sharding import PartitionSpec as P

LANES = 128
HALF = 64
F32 = jnp.float32
BF16 = jnp.bfloat16
MIB = 1024 * 1024
ALL_VMEM = 67043328
ANY = pl.BlockSpec(memory_space=pl.ANY)
VMEM = pl.BlockSpec(memory_space=pltpu.VMEM)
SMEM = pl.BlockSpec(memory_space=pltpu.SMEM)
HBM = pl.BlockSpec(memory_space=pltpu.HBM)


def round_up(value, step):
    return -(-value // step) * step


def factor_columns(scales_ref, live_ref):
    groups = scales_ref.shape[0]
    row = lax.broadcasted_iota(jnp.int32, (groups, LANES), 0)
    lane = lax.broadcasted_iota(jnp.int32, (groups, LANES), 1)
    live = (row * LANES + lane) < live_ref[0]
    factors = scales_ref[...] * live.astype(F32)
    if groups < LANES:
        factors = jnp.concatenate([factors, jnp.zeros((LANES - groups, LANES), F32)], axis=0)
    return factors.T


def dot(left, right, left_dim=1, right_dim=0):
    return lax.dot_general(
        left, right, (((left_dim,), (right_dim,)), ((), ())), preferred_element_type=F32
    )


def offset_rows(index_ref, peers, per_share, share_len):
    groups = index_ref.shape[0]
    table = index_ref[...].astype(F32)
    if groups < LANES:
        table = jnp.concatenate([table, jnp.zeros((LANES - groups, LANES), F32)], axis=0)
    table = table.T
    row = lax.broadcasted_iota(jnp.int32, (LANES, LANES), 0).astype(F32)
    lane = lax.broadcasted_iota(jnp.int32, (LANES, LANES), 1).astype(F32)
    peer_row = lax.broadcasted_iota(jnp.int32, (peers, LANES), 0).astype(F32)
    peer_lane = lax.broadcasted_iota(jnp.int32, (peers, LANES), 1).astype(F32)
    total = jnp.zeros((peers, LANES), F32)
    for group in range(groups):
        peer = jnp.floor((row + (group * LANES + 0.5)) * (1.0 / per_share))
        place = row + group * LANES - peer * per_share
        spread = jnp.where(place == lane, table[:, group : group + 1] - peer * share_len, 0.0)
        owner = jnp.floor((peer_lane + (group * LANES + 0.5)) * (1.0 / per_share))
        chosen = (owner == peer_row).astype(F32)
        total = total + dot(chosen.astype(BF16), spread.astype(BF16))
    return total


def forward_kernel(
    per_share, share_len, rhs_hbm, diag_hbm, codes_hbm, scales_ref, index_ref, live_ref,
    forward_ref, chunks_ref,
    rhs, diag, codes, coupled, packed, sems,
):
    blocks, block_len = diag.shape[0], diag.shape[1]
    rows, rhs_count = codes.shape[0], rhs.shape[0]
    half = per_share // 2
    copies = [pltpu.make_async_copy(rhs_hbm, rhs, sems.at[0])]
    for block in range(blocks):
        copies.append(
            pltpu.make_async_copy(diag_hbm.at[block], diag.at[block], sems.at[1 + block])
        )
    copies.append(pltpu.make_async_copy(codes_hbm, codes, sems.at[1 + blocks]))
    for copy in copies:
        copy.start()
    factors = factor_columns(scales_ref, live_ref)
    offsets = offset_rows(index_ref, rows // per_share, per_share, share_len)
    packed[...] = jnp.zeros_like(packed)
    copies[0].wait()
    for block in range(blocks):
        copies[1 + block].wait()
        columns = slice(block * block_len, (block + 1) * block_len)
        forward_ref[:, columns] = dot(rhs[:, columns], diag[block]).astype(BF16)
    copies[-1].wait()
    for group in range(0, rows, LANES):
        span = slice(group, min(group + LANES, rows))
        count = span.stop - span.start
        value = dot(codes[span, :], forward_ref[...], 1, 1)
        value = value * factors[:count, group // LANES : group // LANES + 1]
        coupled[span, :LANES] = value[:, :LANES]
        tail = value[:, LANES:]
        coupled[span, LANES : LANES + HALF] = tail
        coupled[span, LANES + HALF :] = tail
    low_lane = lax.broadcasted_iota(jnp.int32, (half, LANES), 1) < HALF
    for peer in range(rows // per_share):
        first = peer * per_share
        packed[peer, :per_share, :] = coupled[first : first + per_share, :LANES]
        packed[peer, per_share : per_share + half, :] = jnp.where(
            low_lane,
            coupled[first : first + half, LANES:],
            coupled[first + half : first + per_share, LANES:],
        )
        packed[peer, per_share + half : per_share + half + 1, :] = offsets[peer : peer + 1, :]
    chunks_ref[...] = packed[...].astype(BF16)


def sum_kernel(per_share, chunks_ref, hot_ref, sums_ref, wide, table, total):
    peers, chunk_rows = chunks_ref.shape[0], chunks_ref.shape[1]
    members, own_pad = sums_ref.shape[0], sums_ref.shape[1]
    half = per_share // 2
    wide[...] = chunks_ref[...].astype(F32)
    for peer in range(peers):
        table[peer : peer + 1, :] = wide[peer, per_share + half : per_share + half + 1, :]
    if peers < LANES:
        table[peers:, :] = jnp.zeros((LANES - peers, LANES), F32)
    offsets = table[...].T
    row = lax.broadcasted_iota(jnp.int32, (LANES, LANES), 0)
    tail_row = jnp.logical_and(row >= per_share, row < per_share + half)
    shifts = (
        jnp.where(row < per_share, offsets, -1.0),
        jnp.where(tail_row, pltpu.roll(offsets, per_share, 0), -1.0),
        jnp.where(tail_row, pltpu.roll(offsets, half, 0), -1.0),
    )
    lane = lax.broadcasted_iota(jnp.int32, (chunk_rows, LANES), 1).astype(F32)
    for peer in range(peers):
        span = slice(peer * chunk_rows, (peer + 1) * chunk_rows)
        for part, shifted in enumerate(shifts):
            hit = shifted[:chunk_rows, peer : peer + 1] == lane
            hot_ref[span, part * LANES : (part + 1) * LANES] = hit.astype(F32).astype(BF16)
    values = wide[...].reshape(peers * chunk_rows, LANES).T.astype(BF16)
    result = dot(values, hot_ref[...])
    total[:LANES, :] = result[:, :LANES]
    total[LANES:, :] = result[:HALF, LANES : 2 * LANES] + result[HALF:, 2 * LANES :]
    own = total.shape[0] // members
    if own < own_pad:
        sums_ref[...] = jnp.zeros_like(sums_ref)
    for member in range(members):
        sums_ref[member, :own, :] = total[member * own : (member + 1) * own, :].astype(BF16)


def spread_kernel(own, solved_ref, solution_ref, picker_ref, wide, total):
    members = solved_ref.shape[0]
    wide[...] = solved_ref[...].astype(F32)
    for member in range(members):
        total[member * own : (member + 1) * own, :] = wide[member, :own, :]
    value = total[...]
    tail = value[LANES:, :].astype(BF16)
    nothing = jnp.zeros((HALF, LANES), BF16)
    picker_ref[:, :LANES] = value[:LANES, :].astype(BF16)
    picker_ref[:HALF, LANES : 2 * LANES] = tail
    picker_ref[HALF:, LANES : 2 * LANES] = nothing
    picker_ref[:HALF, 2 * LANES :] = nothing
    picker_ref[HALF:, 2 * LANES :] = tail
    padded = jnp.concatenate([value, jnp.zeros((HALF, LANES), F32)], axis=0)
    flipped = padded.T
    solution_ref[...] = flipped[: solution_ref.shape[0], : solution_ref.shape[1]]


def backward_kernel(
    per_share, chunks_ref, scales_ref, live_ref, forward_ref, codes_hbm, diag_hbm,
    result_ref,
    codes, diag, wide, picked, sems,
):
    blocks, block_len = diag.shape[0], diag.shape[1]
    rows, rhs_count = codes.shape[0], forward_ref.shape[0]
    half = per_share // 2
    copies = [pltpu.make_async_copy(codes_hbm, codes, sems.at[0])]
    for block in range(blocks):
        copies.append(
            pltpu.make_async_copy(diag_hbm.at[block], diag.at[block], sems.at[1 + block])
        )
    for copy in copies:
        copy.start()
    factors = factor_columns(scales_ref, live_ref)
    wide[...] = chunks_ref[...].astype(F32)
    for peer in range(rows // per_share):
        first = peer * per_share
        picked[first : first + per_share, :LANES] = wide[peer, :per_share, :]
        tail = wide[peer, per_share : per_share + half, :]
        picked[first : first + half, LANES:] = tail
        picked[first + half : first + per_share, LANES:] = pltpu.roll(tail, HALF, 1)
    weighted = []
    for group in range(0, rows, LANES):
        span = slice(group, min(group + LANES, rows))
        count = span.stop - span.start
        value = picked[span, :] * factors[:count, group // LANES : group // LANES + 1]
        weighted.append(value.T[:rhs_count].astype(BF16))
    weighted = jnp.concatenate(weighted, axis=1)
    copies[0].wait()
    for block in range(blocks):
        columns = slice(block * block_len, (block + 1) * block_len)
        update = dot(weighted, codes[:, columns])
        misfit = (forward_ref[:, columns].astype(F32) - update).astype(BF16)
        copies[1 + block].wait()
        result_ref[:, columns] = dot(misfit, diag[block], 1, 1).astype(BF16)


def params(limit):
    return pltpu.CompilerParams(vmem_limit_bytes=limit)


def cost(flops, moved):
    return pl.CostEstimate(flops=flops, bytes_accessed=moved, transcendentals=0)


def on_device(rhs_local, diag_inv, codes, row_scales, sep_index, live_rows, rhs_sep, root_inv):
    rhs_count, local_len = rhs_local.shape
    per_dev, block_len = (diag_inv.shape[0], diag_inv.shape[1])
    coupled_rows = codes.shape[0]
    share_len, sep_len = root_inv.shape
    tile_count = lax.axis_size("tile")
    grid_count = lax.axis_size("grid")
    per_share = coupled_rows // tile_count
    chunk_rows = round_up(per_share + per_share // 2 + 1, 16)
    own_rhs = rhs_count // grid_count
    own_pad = round_up(own_rhs, 16)

    groups = -(-coupled_rows // LANES)
    scales = jnp.pad(row_scales, (0, groups * LANES - coupled_rows)).reshape(groups, LANES)
    indices = jnp.pad(sep_index, (0, groups * LANES - coupled_rows)).reshape(groups, LANES)

    forward_flat, chunks = pl.pallas_call(
        functools.partial(forward_kernel, per_share, share_len),
        out_shape=(
            jax.ShapeDtypeStruct((rhs_count, local_len), BF16),
            jax.ShapeDtypeStruct((tile_count, chunk_rows, LANES), BF16),
        ),
        in_specs=[HBM, HBM, HBM, VMEM, VMEM, SMEM],
        out_specs=(VMEM, VMEM),
        scratch_shapes=[
            pltpu.VMEM((rhs_count, local_len), BF16),
            pltpu.VMEM(diag_inv.shape, BF16),
            pltpu.VMEM(codes.shape, BF16),
            pltpu.VMEM((coupled_rows, 2 * LANES), F32),
            pltpu.VMEM((tile_count, chunk_rows, LANES), F32),
            pltpu.SemaphoreType.DMA((2 + per_dev,)),
        ],
        compiler_params=params(ALL_VMEM),
        cost_estimate=cost(2 * rhs_count * local_len * (block_len + coupled_rows), 5 << 20),
        name="forward",
    )(rhs_local, diag_inv, codes, scales, indices, live_rows)
    arrived = lax.all_to_all(chunks, "tile", 0, 0, tiled=True)
    onehot, sums = pl.pallas_call(
        functools.partial(sum_kernel, per_share),
        out_shape=(
            jax.ShapeDtypeStruct((tile_count * chunk_rows, 3 * LANES), BF16),
            jax.ShapeDtypeStruct((grid_count, own_pad, LANES), BF16),
        ),
        in_specs=[VMEM],
        out_specs=(VMEM, VMEM),
        scratch_shapes=[
            pltpu.VMEM((tile_count, chunk_rows, LANES), F32),
            pltpu.VMEM((LANES, LANES), F32),
            pltpu.VMEM((rhs_count, LANES), F32),
        ],
        compiler_params=params(8 * MIB),
        cost_estimate=cost(2 * tile_count * chunk_rows * 3 * LANES * LANES, 1 << 20),
        name="gather_sum",
    )(arrived)
    own_share = lax.all_to_all(sums, "grid", 0, 0, tiled=True).astype(F32).sum(axis=0)
    own_right = lax.dynamic_slice_in_dim(rhs_sep, lax.axis_index("grid") * own_rhs, own_rhs, 0)
    own_right = jnp.pad(own_right, ((0, own_pad - own_rhs), (0, LANES - share_len)))
    residue = (own_right.astype(F32) - own_share)[:, :share_len].astype(BF16)
    spaced = root_inv.reshape(share_len, tile_count, share_len)
    spaced = jnp.pad(spaced, ((0, 0), (0, 0), (0, LANES - share_len)))
    spaced = spaced.reshape(share_len, tile_count * LANES)
    root_part = jnp.dot(residue, spaced, preferred_element_type=F32).astype(BF16)
    root_part = root_part.reshape(own_pad, tile_count, LANES).transpose(1, 0, 2)
    forward_sep = lax.all_to_all(root_part, "tile", 0, 0, tiled=True).astype(F32).sum(axis=0)
    forward_sep = jnp.broadcast_to(
        forward_sep.astype(BF16)[None], (tile_count, own_pad, LANES)
    )
    forward_sep = lax.all_to_all(forward_sep, "tile", 0, 0, tiled=True)
    forward_sep = forward_sep.transpose(1, 0, 2).reshape(own_pad, tile_count * LANES)
    solved = dot(forward_sep, spaced, 1, 1)
    solved = jnp.pad(solved.astype(BF16), ((0, 0), (0, LANES - share_len)))
    solved = jnp.broadcast_to(solved[None], (grid_count, own_pad, LANES))
    solved = lax.all_to_all(solved, "grid", 0, 0, tiled=True)
    solution_sep, picker = pl.pallas_call(
        functools.partial(spread_kernel, own_rhs),
        out_shape=(
            jax.ShapeDtypeStruct((share_len, rhs_count), F32),
            jax.ShapeDtypeStruct((LANES, 3 * LANES), BF16),
        ),
        in_specs=[VMEM],
        out_specs=(VMEM, VMEM),
        scratch_shapes=[
            pltpu.VMEM((grid_count, own_pad, LANES), F32),
            pltpu.VMEM((rhs_count, LANES), F32),
        ],
        compiler_params=params(4 * MIB),
        name="spread",
    )(solved)
    picked = dot(onehot, picker, 1, 1).astype(BF16)
    picked = picked.reshape(tile_count, chunk_rows, LANES)
    picked = lax.all_to_all(picked, "tile", 0, 0, tiled=True)
    result = pl.pallas_call(
        functools.partial(backward_kernel, per_share),
        out_shape=jax.ShapeDtypeStruct((rhs_count, local_len), BF16),
        in_specs=[VMEM, VMEM, SMEM, VMEM, ANY, ANY],
        out_specs=VMEM,
        scratch_shapes=[
            pltpu.VMEM(codes.shape, BF16),
            pltpu.VMEM(diag_inv.shape, BF16),
            pltpu.VMEM((tile_count, chunk_rows, LANES), F32),
            pltpu.VMEM((coupled_rows, 2 * LANES), F32),
            pltpu.SemaphoreType.DMA((1 + per_dev,)),
        ],
        compiler_params=params(16 * MIB),
        cost_estimate=cost(2 * rhs_count * local_len * (block_len + coupled_rows), 5 << 20),
        name="backward",
    )(picked, scales, live_rows, forward_flat, codes, diag_inv)
    return (result, solution_sep.T)


def solution(mesh):
    return jax.shard_map(
        on_device,
        mesh=mesh,
        in_specs=(
            P(None, ("grid", "tile")),
            P(("grid", "tile"), None, None),
            P(("grid", "tile"), None),
            P(("grid", "tile")),
            P(("grid", "tile")),
            P(("grid", "tile")),
            P(None, "tile"),
            P("tile", None),
        ),
        out_specs=(P(None, ("grid", "tile")), P(None, "tile")),
        check_vma=False,
    )
```

```python
import functools

import jax
import jax.numpy as jnp
from jax import lax
from jax.experimental import pallas as pl
from jax.experimental.pallas import tpu as pltpu
from jax.sharding import PartitionSpec as P

LANES = 128
HALF = 64
SPLIT = 80
F32 = jnp.float32
BF16 = jnp.bfloat16
MIB = 1024 * 1024
ALL_VMEM = 67043328
ANY = pl.BlockSpec(memory_space=pl.ANY)
VMEM = pl.BlockSpec(memory_space=pltpu.VMEM)
SMEM = pl.BlockSpec(memory_space=pltpu.SMEM)
HBM = pl.BlockSpec(memory_space=pltpu.HBM)


def round_up(value, step):
    return -(-value // step) * step


def factor_columns(scales_ref, live_ref):
    groups = scales_ref.shape[0]
    row = lax.broadcasted_iota(jnp.int32, (groups, LANES), 0)
    lane = lax.broadcasted_iota(jnp.int32, (groups, LANES), 1)
    live = (row * LANES + lane) < live_ref[0]
    factors = scales_ref[...] * live.astype(F32)
    if groups < LANES:
        factors = jnp.concatenate([factors, jnp.zeros((LANES - groups, LANES), F32)], axis=0)
    return factors.T


def dot(left, right, left_dim=1, right_dim=0):
    return lax.dot_general(
        left, right, (((left_dim,), (right_dim,)), ((), ())), preferred_element_type=F32
    )


def offset_rows(index_ref, peers, per_share, share_len):
    groups = index_ref.shape[0]
    table = index_ref[...].astype(F32)
    if groups < LANES:
        table = jnp.concatenate([table, jnp.zeros((LANES - groups, LANES), F32)], axis=0)
    table = table.T
    row = lax.broadcasted_iota(jnp.int32, (LANES, LANES), 0).astype(F32)
    lane = lax.broadcasted_iota(jnp.int32, (LANES, LANES), 1).astype(F32)
    peer_row = lax.broadcasted_iota(jnp.int32, (peers, LANES), 0).astype(F32)
    peer_lane = lax.broadcasted_iota(jnp.int32, (peers, LANES), 1).astype(F32)
    total = jnp.zeros((peers, LANES), F32)
    for group in range(groups):
        peer = jnp.floor((row + (group * LANES + 0.5)) * (1.0 / per_share))
        place = row + group * LANES - peer * per_share
        spread = jnp.where(place == lane, table[:, group : group + 1] - peer * share_len, 0.0)
        owner = jnp.floor((peer_lane + (group * LANES + 0.5)) * (1.0 / per_share))
        chosen = (owner == peer_row).astype(F32)
        total = total + dot(chosen.astype(BF16), spread.astype(BF16))
    return total


def forward_kernel(
    per_share, share_len, rhs_hbm, diag_hbm, codes_hbm, scales_ref, index_ref, live_ref,
    forward_ref, chunks_ref,
    rhs, diag, codes, coupled, packed, sems,
):
    blocks, block_len = diag.shape[0], diag.shape[1]
    rows, rhs_count = codes.shape[0], rhs.shape[0]
    half = per_share // 2
    copies = [pltpu.make_async_copy(rhs_hbm, rhs, sems.at[0])]
    for block in range(blocks):
        copies.append(
            pltpu.make_async_copy(diag_hbm.at[block], diag.at[block], sems.at[1 + block])
        )
    copies.append(pltpu.make_async_copy(codes_hbm, codes, sems.at[1 + blocks]))
    for copy in copies:
        copy.start()
    factors = factor_columns(scales_ref, live_ref)
    offsets = offset_rows(index_ref, rows // per_share, per_share, share_len)
    packed[...] = jnp.zeros_like(packed)
    copies[0].wait()
    for block in range(blocks):
        copies[1 + block].wait()
        columns = slice(block * block_len, (block + 1) * block_len)
        forward_ref[:, columns] = dot(rhs[:, columns], diag[block]).astype(BF16)
    copies[-1].wait()
    coupled_sums = dot(codes[...], forward_ref[...], 1, 1)
    for group in range(0, rows, LANES):
        span = slice(group, min(group + LANES, rows))
        count = span.stop - span.start
        value = coupled_sums[span, :] * factors[:count, group // LANES : group // LANES + 1]
        coupled[span, :LANES] = value[:, :LANES]
        tail = value[:, LANES:]
        coupled[span, LANES : LANES + HALF] = tail
        coupled[span, LANES + HALF :] = tail
    low_lane = lax.broadcasted_iota(jnp.int32, (half, LANES), 1) < HALF
    for peer in range(rows // per_share):
        first = peer * per_share
        packed[peer, :per_share, :] = coupled[first : first + per_share, :LANES]
        packed[peer, per_share : per_share + half, :] = jnp.where(
            low_lane,
            coupled[first : first + half, LANES:],
            coupled[first + half : first + per_share, LANES:],
        )
        packed[peer, per_share + half : per_share + half + 1, :] = offsets[peer : peer + 1, :]
    chunks_ref[...] = packed[...].astype(BF16)


def sum_kernel(per_share, chunks_ref, hot_ref, sums_ref, wide, table, total, early, late):
    peers, chunk_rows = chunks_ref.shape[0], chunks_ref.shape[1]
    members, own_pad = sums_ref.shape[0], sums_ref.shape[1]
    half = per_share // 2
    wide[...] = chunks_ref[...].astype(F32)
    for peer in range(peers):
        table[peer : peer + 1, :] = wide[peer, per_share + half : per_share + half + 1, :]
    if peers < LANES:
        table[peers:, :] = jnp.zeros((LANES - peers, LANES), F32)
    offsets = table[...].T
    row = lax.broadcasted_iota(jnp.int32, (LANES, LANES), 0)
    tail_row = jnp.logical_and(row >= per_share, row < per_share + half)
    shifts = (
        jnp.where(row < per_share, offsets, -1.0),
        jnp.where(tail_row, pltpu.roll(offsets, per_share, 0), -1.0),
        jnp.where(tail_row, pltpu.roll(offsets, half, 0), -1.0),
    )
    lane = lax.broadcasted_iota(jnp.int32, (chunk_rows, LANES), 1).astype(F32)
    for peer in range(peers):
        span = slice(peer * chunk_rows, (peer + 1) * chunk_rows)
        for part, shifted in enumerate(shifts):
            hit = shifted[:chunk_rows, peer : peer + 1] == lane
            hot_ref[span, part * LANES : (part + 1) * LANES] = hit.astype(F32).astype(BF16)
    values = wide[...].reshape(peers * chunk_rows, LANES).T.astype(BF16)
    result = dot(values, hot_ref[...])
    total[:LANES, :] = result[:, :LANES]
    total[LANES:, :] = result[:HALF, LANES : 2 * LANES] + result[HALF:, 2 * LANES :]
    value = total[...]
    early[...] = pltpu.roll(value, SPLIT, 1)
    late[...] = pltpu.roll(value, SPLIT // 2, 1)
    quad = own_pad // 2
    lane = lax.broadcasted_iota(jnp.int32, (quad, LANES), 1)
    for member in range(members):
        first = member * 3 * quad
        for part, moved in enumerate((early, late)):
            extra = jnp.where(lane < SPLIT * 3 // 2, moved[first + 2 * quad : first + 3 * quad, :], 0.0)
            begin = first + part * quad
            sums_ref[member, part * quad : (part + 1) * quad, :] = jnp.where(
                lane < SPLIT, total[begin : begin + quad, :], extra
            )


def weights_kernel(root_ref, weights_ref):
    share_len, sep_len = root_ref.shape
    lane = lax.broadcasted_iota(jnp.int32, (share_len, LANES), 1)
    beside = jnp.logical_and(lane >= SPLIT, lane < SPLIT * 3 // 2)
    weights_ref[3 * share_len :, :] = jnp.zeros_like(weights_ref[3 * share_len :, :])
    for peer in range(sep_len // share_len):
        base = peer * share_len // LANES * LANES
        shift = peer * share_len - base
        width = LANES if shift + share_len <= LANES else 2 * LANES
        block = root_ref[:, base : base + width].astype(F32)
        if shift:
            block = pltpu.roll(block, width - shift, 1)
        block = block[:, :LANES]
        columns = slice(peer * LANES, (peer + 1) * LANES)
        plain = jnp.where(lane < SPLIT, block, 0.0)
        first = jnp.where(beside, pltpu.roll(block, SPLIT, 1), 0.0)
        second = jnp.where(beside, pltpu.roll(block, SPLIT // 2, 1), 0.0)
        weights_ref[:share_len, columns] = plain.astype(BF16)
        weights_ref[share_len : 2 * share_len, columns] = first.astype(BF16)
        weights_ref[2 * share_len : 3 * share_len, columns] = second.astype(BF16)


def root_forward_kernel(sums_ref, right_ref, weights_ref, parts_ref):
    gathered = jnp.sum(sums_ref[...], axis=0)
    residue = (right_ref[...] - gathered).astype(BF16).astype(F32)
    row = lax.broadcasted_iota(jnp.int32, residue.shape, 0)
    lane = lax.broadcasted_iota(jnp.int32, residue.shape, 1)
    top = row < 4
    near = pltpu.roll(residue, LANES - SPLIT, 1)
    far = pltpu.roll(residue, LANES - SPLIT // 2, 1)
    upper = jnp.where(lane < SPLIT // 2, near, pltpu.roll(far, 4, 0))
    lower = jnp.where(lane < SPLIT // 2, pltpu.roll(near, 4, 0), far)
    whole = lane < SPLIT
    upper = pltpu.roll(jnp.where(jnp.logical_and(whole, top), upper, 0.0), SPLIT, 1)
    lower = jnp.where(jnp.logical_and(whole, jnp.logical_not(top)), lower, 0.0)
    lower = pltpu.roll(lower, 2 * SPLIT - LANES, 1)
    left = jnp.where(whole, residue, upper)
    right = jnp.where(lane < 2 * SPLIT - LANES, upper, lower)
    operand = jnp.concatenate([left, right], axis=1).astype(BF16)
    result = dot(operand, weights_ref[...]).astype(BF16)
    for peer in range(parts_ref.shape[0]):
        parts_ref[peer] = result[:, peer * LANES : (peer + 1) * LANES]


def root_backward_kernel(forward_ref, weights_ref, solved_ref):
    peers = forward_ref.shape[0]
    operand = jnp.concatenate([forward_ref[peer] for peer in range(peers)], axis=1)
    result = dot(operand, weights_ref[...], 1, 1)
    left, right = result[:, :LANES], result[:, LANES:]
    row = lax.broadcasted_iota(jnp.int32, left.shape, 0)
    lane = lax.broadcasted_iota(jnp.int32, left.shape, 1)
    gap = LANES - SPLIT
    first = jnp.where(lane < gap, pltpu.roll(left, gap, 1), pltpu.roll(right, gap, 1))
    second = pltpu.roll(right, LANES - (2 * SPLIT - LANES), 1)
    third = first + pltpu.roll(second, 4, 0)
    beside = jnp.where(
        row < 4, pltpu.roll(third, SPLIT, 1), pltpu.roll(pltpu.roll(third, SPLIT // 2, 1), 4, 0)
    )
    packed = jnp.where(lane < SPLIT, left, jnp.where(lane < SPLIT * 3 // 2, beside, 0.0))
    solved_ref[...] = jnp.broadcast_to(packed.astype(BF16)[None], solved_ref.shape)


def spread_kernel(solved_ref, hot_ref, solution_ref, picked_ref, wide, total, picker):
    members, rows = solved_ref.shape[0], solved_ref.shape[1]
    quad = rows // 2
    plain = solved_ref[...].astype(F32).reshape(members * rows, LANES)
    wide[0] = plain
    wide[1] = pltpu.roll(plain, LANES - SPLIT, 1)
    wide[2] = pltpu.roll(plain, LANES - SPLIT // 2, 1)
    lane = lax.broadcasted_iota(jnp.int32, (quad, LANES), 1)
    for member in range(members):
        first, place = member * rows, member * 3 * quad
        total[place : place + rows, :] = wide[0, first : first + rows, :]
        total[place + rows : place + rows + quad, :] = jnp.where(
            lane < SPLIT // 2,
            wide[1, first : first + quad, :],
            wide[2, first + quad : first + rows, :],
        )
    value = jnp.where(lax.broadcasted_iota(jnp.int32, total.shape, 1) < SPLIT, total[...], 0.0)
    tail = value[LANES:, :].astype(BF16)
    nothing = jnp.zeros((HALF, LANES), BF16)
    picker[:, :LANES] = value[:LANES, :].astype(BF16)
    picker[:HALF, LANES : 2 * LANES] = tail
    picker[HALF:, LANES : 2 * LANES] = nothing
    picker[:HALF, 2 * LANES :] = nothing
    picker[HALF:, 2 * LANES :] = tail
    picked = dot(hot_ref[...], picker[...], 1, 1).astype(BF16)
    picked_ref[...] = picked.reshape(picked_ref.shape)
    padded = jnp.concatenate([value, jnp.zeros((HALF, LANES), F32)], axis=0)
    flipped = padded.T
    solution_ref[...] = flipped[: solution_ref.shape[0], : solution_ref.shape[1]]


def backward_kernel(
    per_share, chunks_ref, scales_ref, live_ref, forward_ref, codes_hbm, diag_hbm,
    result_ref,
    codes, diag, wide, picked, sems,
):
    blocks, block_len = diag.shape[0], diag.shape[1]
    rows, rhs_count = codes.shape[0], forward_ref.shape[0]
    half = per_share // 2
    copies = [pltpu.make_async_copy(codes_hbm, codes, sems.at[0])]
    for block in range(blocks):
        copies.append(
            pltpu.make_async_copy(diag_hbm.at[block], diag.at[block], sems.at[1 + block])
        )
    for copy in copies:
        copy.start()
    factors = factor_columns(scales_ref, live_ref)
    wide[...] = chunks_ref[...].astype(F32)
    for peer in range(rows // per_share):
        first = peer * per_share
        picked[first : first + per_share, :LANES] = wide[peer, :per_share, :]
        tail = wide[peer, per_share : per_share + half, :]
        picked[first : first + half, LANES:] = tail
        picked[first + half : first + per_share, LANES:] = pltpu.roll(tail, HALF, 1)
    weighted = []
    for group in range(0, rows, LANES):
        span = slice(group, min(group + LANES, rows))
        count = span.stop - span.start
        value = picked[span, :] * factors[:count, group // LANES : group // LANES + 1]
        weighted.append(value.T[:rhs_count].astype(BF16))
    weighted = jnp.concatenate(weighted, axis=1)
    copies[0].wait()
    for block in range(blocks):
        columns = slice(block * block_len, (block + 1) * block_len)
        update = dot(weighted, codes[:, columns])
        misfit = (forward_ref[:, columns].astype(F32) - update).astype(BF16)
        copies[1 + block].wait()
        result_ref[:, columns] = dot(misfit, diag[block], 1, 1).astype(BF16)


def params(limit):
    return pltpu.CompilerParams(vmem_limit_bytes=limit)


def cost(flops, moved):
    return pl.CostEstimate(flops=flops, bytes_accessed=moved, transcendentals=0)


def on_device(rhs_local, diag_inv, codes, row_scales, sep_index, live_rows, rhs_sep, root_inv):
    rhs_count, local_len = rhs_local.shape
    per_dev, block_len = (diag_inv.shape[0], diag_inv.shape[1])
    coupled_rows = codes.shape[0]
    share_len, sep_len = root_inv.shape
    tile_count = lax.axis_size("tile")
    grid_count = lax.axis_size("grid")
    per_share = coupled_rows // tile_count
    chunk_rows = round_up(per_share + per_share // 2 + 1, 16)
    own_rhs = rhs_count // grid_count
    own_pad = own_rhs * 2 // 3
    assert own_rhs == 12 and share_len == SPLIT and rhs_count == LANES + HALF

    groups = -(-coupled_rows // LANES)
    scales = jnp.pad(row_scales, (0, groups * LANES - coupled_rows)).reshape(groups, LANES)
    indices = jnp.pad(sep_index, (0, groups * LANES - coupled_rows)).reshape(groups, LANES)

    forward_flat, chunks = pl.pallas_call(
        functools.partial(forward_kernel, per_share, share_len),
        out_shape=(
            jax.ShapeDtypeStruct((rhs_count, local_len), BF16),
            jax.ShapeDtypeStruct((tile_count, chunk_rows, LANES), BF16),
        ),
        in_specs=[HBM, HBM, HBM, VMEM, VMEM, SMEM],
        out_specs=(VMEM, VMEM),
        scratch_shapes=[
            pltpu.VMEM((rhs_count, local_len), BF16),
            pltpu.VMEM(diag_inv.shape, BF16),
            pltpu.VMEM(codes.shape, BF16),
            pltpu.VMEM((coupled_rows, 2 * LANES), F32),
            pltpu.VMEM((tile_count, chunk_rows, LANES), F32),
            pltpu.SemaphoreType.DMA((2 + per_dev,)),
        ],
        compiler_params=params(ALL_VMEM),
        cost_estimate=cost(2 * rhs_count * local_len * (block_len + coupled_rows), 5 << 20),
        name="forward",
    )(rhs_local, diag_inv, codes, scales, indices, live_rows)
    arrived = lax.all_to_all(chunks, "tile", 0, 0, tiled=True)
    onehot, sums = pl.pallas_call(
        functools.partial(sum_kernel, per_share),
        out_shape=(
            jax.ShapeDtypeStruct((tile_count * chunk_rows, 3 * LANES), BF16),
            jax.ShapeDtypeStruct((grid_count, own_pad, LANES), F32),
        ),
        in_specs=[VMEM],
        out_specs=(VMEM, VMEM),
        scratch_shapes=[
            pltpu.VMEM((tile_count, chunk_rows, LANES), F32),
            pltpu.VMEM((LANES, LANES), F32),
            pltpu.VMEM((rhs_count, LANES), F32),
            pltpu.VMEM((rhs_count, LANES), F32),
            pltpu.VMEM((rhs_count, LANES), F32),
        ],
        compiler_params=params(8 * MIB),
        cost_estimate=cost(2 * tile_count * chunk_rows * 3 * LANES * LANES, 1 << 20),
        name="gather_sum",
    )(arrived)
    weight_rows = round_up(3 * share_len, LANES)
    weights = pl.pallas_call(
        weights_kernel,
        out_shape=jax.ShapeDtypeStruct((weight_rows, tile_count * LANES), BF16),
        in_specs=[VMEM],
        out_specs=VMEM,
        compiler_params=params(4 * MIB),
        cost_estimate=cost(share_len * sep_len * 16, 3 << 20),
        name="weights",
    )(root_inv)
    arrived_sums = lax.all_to_all(sums, "grid", 0, 0, tiled=True)
    right = lax.dynamic_slice_in_dim(rhs_sep, lax.axis_index("grid") * own_rhs, own_rhs, 0)
    beside = jnp.concatenate([right[own_pad:, : SPLIT // 2], right[own_pad:, SPLIT // 2 :]], axis=0)
    right = jnp.concatenate([right[:own_pad], beside], axis=1).astype(F32)
    right = jnp.pad(right, ((0, 0), (0, LANES - right.shape[1])))
    root_part = pl.pallas_call(
        root_forward_kernel,
        out_shape=jax.ShapeDtypeStruct((tile_count, own_pad, LANES), BF16),
        in_specs=[VMEM, VMEM, VMEM],
        out_specs=VMEM,
        compiler_params=params(4 * MIB),
        cost_estimate=cost(2 * own_pad * weight_rows * tile_count * LANES, 2 << 20),
        name="root_forward",
    )(arrived_sums, right, weights)
    forward_sep = lax.all_to_all(root_part, "tile", 0, 0, tiled=True).astype(F32).sum(axis=0)
    forward_sep = jnp.broadcast_to(forward_sep.astype(BF16)[None], (tile_count, own_pad, LANES))
    forward_sep = lax.all_to_all(forward_sep, "tile", 0, 0, tiled=True)
    solved = pl.pallas_call(
        root_backward_kernel,
        out_shape=jax.ShapeDtypeStruct((grid_count, own_pad, LANES), BF16),
        in_specs=[VMEM, VMEM],
        out_specs=VMEM,
        compiler_params=params(4 * MIB),
        cost_estimate=cost(2 * own_pad * weight_rows * tile_count * LANES, 2 << 20),
        name="root_backward",
    )(forward_sep, weights)
    solved = lax.all_to_all(solved, "grid", 0, 0, tiled=True)
    solution_sep, picked = pl.pallas_call(
        spread_kernel,
        out_shape=(
            jax.ShapeDtypeStruct((share_len, rhs_count), F32),
            jax.ShapeDtypeStruct((tile_count, chunk_rows, LANES), BF16),
        ),
        in_specs=[VMEM, VMEM],
        out_specs=(VMEM, VMEM),
        scratch_shapes=[
            pltpu.VMEM((3, grid_count * own_pad, LANES), F32),
            pltpu.VMEM((rhs_count, LANES), F32),
            pltpu.VMEM((LANES, 3 * LANES), BF16),
        ],
        compiler_params=params(6 * MIB),
        cost_estimate=cost(2 * tile_count * chunk_rows * 3 * LANES * LANES, 1 << 20),
        name="spread",
    )(solved, onehot)
    picked = lax.all_to_all(picked, "tile", 0, 0, tiled=True)
    result = pl.pallas_call(
        functools.partial(backward_kernel, per_share),
        out_shape=jax.ShapeDtypeStruct((rhs_count, local_len), BF16),
        in_specs=[VMEM, VMEM, SMEM, VMEM, ANY, ANY],
        out_specs=VMEM,
        scratch_shapes=[
            pltpu.VMEM(codes.shape, BF16),
            pltpu.VMEM(diag_inv.shape, BF16),
            pltpu.VMEM((tile_count, chunk_rows, LANES), F32),
            pltpu.VMEM((coupled_rows, 2 * LANES), F32),
            pltpu.SemaphoreType.DMA((1 + per_dev,)),
        ],
        compiler_params=params(16 * MIB),
        cost_estimate=cost(2 * rhs_count * local_len * (block_len + coupled_rows), 5 << 20),
        name="backward",
    )(picked, scales, live_rows, forward_flat, codes, diag_inv)
    return (result, solution_sep.T)


def solution(mesh):
    return jax.shard_map(
        on_device,
        mesh=mesh,
        in_specs=(
            P(None, ("grid", "tile")),
            P(("grid", "tile"), None, None),
            P(("grid", "tile"), None),
            P(("grid", "tile")),
            P(("grid", "tile")),
            P(("grid", "tile")),
            P(None, "tile"),
            P("tile", None),
        ),
        out_specs=(P(None, ("grid", "tile")), P(None, "tile")),
        check_vma=False,
    )
```

```python
import functools

import jax
import jax.numpy as jnp
from jax import lax
from jax.experimental import pallas as pl
from jax.experimental.pallas import tpu as pltpu
from jax.sharding import PartitionSpec as P

LANES = 128
HALF = 64
SPLIT = 80
F32 = jnp.float32
BF16 = jnp.bfloat16
MIB = 1024 * 1024
ALL_VMEM = 67043328
VMEM = pl.BlockSpec(memory_space=pltpu.VMEM)
SMEM = pl.BlockSpec(memory_space=pltpu.SMEM)
HBM = pl.BlockSpec(memory_space=pltpu.HBM)


def round_up(value, step):
    return -(-value // step) * step


def factor_columns(scales_ref, live_ref):
    groups = scales_ref.shape[0]
    row = lax.broadcasted_iota(jnp.int32, (groups, LANES), 0)
    lane = lax.broadcasted_iota(jnp.int32, (groups, LANES), 1)
    live = (row * LANES + lane) < live_ref[0]
    factors = scales_ref[...] * live.astype(F32)
    if groups < LANES:
        factors = jnp.concatenate([factors, jnp.zeros((LANES - groups, LANES), F32)], axis=0)
    return factors.T


def dot(left, right, left_dim=1, right_dim=0):
    return lax.dot_general(
        left, right, (((left_dim,), (right_dim,)), ((), ())), preferred_element_type=F32
    )


def offset_rows(index_ref, peers, per_share, share_len):
    groups = index_ref.shape[0]
    table = index_ref[...].astype(F32)
    if groups < LANES:
        table = jnp.concatenate([table, jnp.zeros((LANES - groups, LANES), F32)], axis=0)
    table = table.T
    row = lax.broadcasted_iota(jnp.int32, (LANES, LANES), 0).astype(F32)
    lane = lax.broadcasted_iota(jnp.int32, (LANES, LANES), 1).astype(F32)
    peer_row = lax.broadcasted_iota(jnp.int32, (peers, LANES), 0).astype(F32)
    peer_lane = lax.broadcasted_iota(jnp.int32, (peers, LANES), 1).astype(F32)
    total = jnp.zeros((peers, LANES), F32)
    for group in range(groups):
        peer = jnp.floor((row + (group * LANES + 0.5)) * (1.0 / per_share))
        place = row + group * LANES - peer * per_share
        spread = jnp.where(place == lane, table[:, group : group + 1] - peer * share_len, 0.0)
        owner = jnp.floor((peer_lane + (group * LANES + 0.5)) * (1.0 / per_share))
        chosen = (owner == peer_row).astype(F32)
        total = total + dot(chosen.astype(BF16), spread.astype(BF16))
    return total


def forward_kernel(
    per_share, share_len, rhs_hbm, diag_hbm, codes_hbm, scales_ref, index_ref, live_ref,
    forward_ref, chunks_ref,
    rhs, diag, codes, coupled, packed, sems,
):
    blocks, block_len = diag.shape[0], diag.shape[1]
    rows, rhs_count = codes.shape[0], rhs.shape[0]
    half = per_share // 2
    copies = [pltpu.make_async_copy(rhs_hbm, rhs, sems.at[0])]
    for block in range(blocks):
        copies.append(
            pltpu.make_async_copy(diag_hbm.at[block], diag.at[block], sems.at[1 + block])
        )
    copies.append(pltpu.make_async_copy(codes_hbm, codes, sems.at[1 + blocks]))
    for copy in copies[:-1]:
        copy.start()
    factors = factor_columns(scales_ref, live_ref)
    offsets = offset_rows(index_ref, rows // per_share, per_share, share_len)
    packed[...] = jnp.zeros_like(packed)
    copies[0].wait()
    copies[-1].start()
    for block in range(blocks):
        copies[1 + block].wait()
        columns = slice(block * block_len, (block + 1) * block_len)
        forward_ref[:, columns] = dot(rhs[:, columns], diag[block]).astype(BF16)
    copies[-1].wait()
    coupled_sums = dot(codes[...], forward_ref[...], 1, 1)
    for group in range(0, rows, LANES):
        span = slice(group, min(group + LANES, rows))
        count = span.stop - span.start
        value = coupled_sums[span, :] * factors[:count, group // LANES : group // LANES + 1]
        coupled[span, :LANES] = value[:, :LANES]
        tail = value[:, LANES:]
        coupled[span, LANES : LANES + HALF] = tail
        coupled[span, LANES + HALF :] = tail
    low_lane = lax.broadcasted_iota(jnp.int32, (half, LANES), 1) < HALF
    for peer in range(rows // per_share):
        first = peer * per_share
        packed[peer, :per_share, :] = coupled[first : first + per_share, :LANES]
        packed[peer, per_share : per_share + half, :] = jnp.where(
            low_lane,
            coupled[first : first + half, LANES:],
            coupled[first + half : first + per_share, LANES:],
        )
        packed[peer, per_share + half : per_share + half + 1, :] = offsets[peer : peer + 1, :]
    chunks_ref[...] = packed[...].astype(BF16)


def sum_kernel(per_share, chunks_ref, hot_ref, sums_ref, wide, table, total, early, late):
    peers, chunk_rows = chunks_ref.shape[0], chunks_ref.shape[1]
    members, own_pad = sums_ref.shape[0], sums_ref.shape[1]
    half = per_share // 2
    wide[...] = chunks_ref[...].astype(F32)
    for peer in range(peers):
        table[peer : peer + 1, :] = wide[peer, per_share + half : per_share + half + 1, :]
    if peers < LANES:
        table[peers:, :] = jnp.zeros((LANES - peers, LANES), F32)
    offsets = table[...].T
    row = lax.broadcasted_iota(jnp.int32, (LANES, LANES), 0)
    tail_row = jnp.logical_and(row >= per_share, row < per_share + half)
    shifts = (
        jnp.where(row < per_share, offsets, -1.0),
        jnp.where(tail_row, pltpu.roll(offsets, per_share, 0), -1.0),
        jnp.where(tail_row, pltpu.roll(offsets, half, 0), -1.0),
    )
    lane = lax.broadcasted_iota(jnp.int32, (chunk_rows, LANES), 1).astype(F32)
    for peer in range(peers):
        span = slice(peer * chunk_rows, (peer + 1) * chunk_rows)
        for part, shifted in enumerate(shifts):
            hit = shifted[:chunk_rows, peer : peer + 1] == lane
            hot_ref[span, part * LANES : (part + 1) * LANES] = hit.astype(F32).astype(BF16)
    values = wide[...].reshape(peers * chunk_rows, LANES).T.astype(BF16)
    result = dot(values, hot_ref[...])
    total[:LANES, :] = result[:, :LANES]
    total[LANES:, :] = result[:HALF, LANES : 2 * LANES] + result[HALF:, 2 * LANES :]
    value = total[...]
    early[...] = pltpu.roll(value, SPLIT, 1)
    late[...] = pltpu.roll(value, SPLIT // 2, 1)
    quad = own_pad // 2
    lane = lax.broadcasted_iota(jnp.int32, (quad, LANES), 1)
    for member in range(members):
        first = member * 3 * quad
        for part, moved in enumerate((early, late)):
            extra = jnp.where(lane < SPLIT * 3 // 2, moved[first + 2 * quad : first + 3 * quad, :], 0.0)
            begin = first + part * quad
            sums_ref[member, part * quad : (part + 1) * quad, :] = jnp.where(
                lane < SPLIT, total[begin : begin + quad, :], extra
            )


def weights_kernel(root_ref, weights_ref):
    share_len, sep_len = root_ref.shape
    lane = lax.broadcasted_iota(jnp.int32, (share_len, LANES), 1)
    beside = jnp.logical_and(lane >= SPLIT, lane < SPLIT * 3 // 2)
    weights_ref[3 * share_len :, :] = jnp.zeros_like(weights_ref[3 * share_len :, :])
    for peer in range(sep_len // share_len):
        base = peer * share_len // LANES * LANES
        shift = peer * share_len - base
        width = LANES if shift + share_len <= LANES else 2 * LANES
        block = root_ref[:, base : base + width].astype(F32)
        if shift:
            block = pltpu.roll(block, width - shift, 1)
        block = block[:, :LANES]
        columns = slice(peer * LANES, (peer + 1) * LANES)
        plain = jnp.where(lane < SPLIT, block, 0.0)
        first = jnp.where(beside, pltpu.roll(block, SPLIT, 1), 0.0)
        second = jnp.where(beside, pltpu.roll(block, SPLIT // 2, 1), 0.0)
        weights_ref[:share_len, columns] = plain.astype(BF16)
        weights_ref[share_len : 2 * share_len, columns] = first.astype(BF16)
        weights_ref[2 * share_len : 3 * share_len, columns] = second.astype(BF16)


def root_forward_kernel(sums_ref, right_ref, weights_ref, parts_ref):
    gathered = jnp.sum(sums_ref[...], axis=0)
    residue = (right_ref[...] - gathered).astype(BF16).astype(F32)
    row = lax.broadcasted_iota(jnp.int32, residue.shape, 0)
    lane = lax.broadcasted_iota(jnp.int32, residue.shape, 1)
    top = row < 4
    near = pltpu.roll(residue, LANES - SPLIT, 1)
    far = pltpu.roll(residue, LANES - SPLIT // 2, 1)
    upper = jnp.where(lane < SPLIT // 2, near, pltpu.roll(far, 4, 0))
    lower = jnp.where(lane < SPLIT // 2, pltpu.roll(near, 4, 0), far)
    whole = lane < SPLIT
    upper = pltpu.roll(jnp.where(jnp.logical_and(whole, top), upper, 0.0), SPLIT, 1)
    lower = jnp.where(jnp.logical_and(whole, jnp.logical_not(top)), lower, 0.0)
    lower = pltpu.roll(lower, 2 * SPLIT - LANES, 1)
    left = jnp.where(whole, residue, upper)
    right = jnp.where(lane < 2 * SPLIT - LANES, upper, lower)
    operand = jnp.concatenate([left, right], axis=1).astype(BF16)
    result = dot(operand, weights_ref[...]).astype(BF16)
    for peer in range(parts_ref.shape[0]):
        parts_ref[peer] = result[:, peer * LANES : (peer + 1) * LANES]


def root_middle_kernel(parts_ref, forward_ref):
    total = jnp.sum(parts_ref[...].astype(F32), axis=0).astype(BF16)
    forward_ref[...] = jnp.broadcast_to(total[None], forward_ref.shape)


def root_backward_kernel(forward_ref, weights_ref, solved_ref):
    peers = forward_ref.shape[0]
    operand = jnp.concatenate([forward_ref[peer] for peer in range(peers)], axis=1)
    result = dot(operand, weights_ref[...], 1, 1)
    left, right = result[:, :LANES], result[:, LANES:]
    row = lax.broadcasted_iota(jnp.int32, left.shape, 0)
    lane = lax.broadcasted_iota(jnp.int32, left.shape, 1)
    gap = LANES - SPLIT
    first = jnp.where(lane < gap, pltpu.roll(left, gap, 1), pltpu.roll(right, gap, 1))
    second = pltpu.roll(right, LANES - (2 * SPLIT - LANES), 1)
    third = first + pltpu.roll(second, 4, 0)
    beside = jnp.where(
        row < 4, pltpu.roll(third, SPLIT, 1), pltpu.roll(pltpu.roll(third, SPLIT // 2, 1), 4, 0)
    )
    packed = jnp.where(lane < SPLIT, left, jnp.where(lane < SPLIT * 3 // 2, beside, 0.0))
    solved_ref[...] = jnp.broadcast_to(packed.astype(BF16)[None], solved_ref.shape)


def spread_kernel(solved_ref, hot_ref, solution_ref, picked_ref, wide, total, picker):
    members, rows = solved_ref.shape[0], solved_ref.shape[1]
    quad = rows // 2
    plain = solved_ref[...].astype(F32).reshape(members * rows, LANES)
    wide[0] = plain
    wide[1] = pltpu.roll(plain, LANES - SPLIT, 1)
    wide[2] = pltpu.roll(plain, LANES - SPLIT // 2, 1)
    lane = lax.broadcasted_iota(jnp.int32, (quad, LANES), 1)
    for member in range(members):
        first, place = member * rows, member * 3 * quad
        total[place : place + rows, :] = wide[0, first : first + rows, :]
        total[place + rows : place + rows + quad, :] = jnp.where(
            lane < SPLIT // 2,
            wide[1, first : first + quad, :],
            wide[2, first + quad : first + rows, :],
        )
    value = jnp.where(lax.broadcasted_iota(jnp.int32, total.shape, 1) < SPLIT, total[...], 0.0)
    tail = value[LANES:, :].astype(BF16)
    nothing = jnp.zeros((HALF, LANES), BF16)
    picker[:, :LANES] = value[:LANES, :].astype(BF16)
    picker[:HALF, LANES : 2 * LANES] = tail
    picker[HALF:, LANES : 2 * LANES] = nothing
    picker[:HALF, 2 * LANES :] = nothing
    picker[HALF:, 2 * LANES :] = tail
    picked = dot(hot_ref[...], picker[...], 1, 1).astype(BF16)
    picked_ref[...] = picked.reshape(picked_ref.shape)
    padded = jnp.concatenate([value, jnp.zeros((HALF, LANES), F32)], axis=0)
    flipped = padded.T
    solution_ref[...] = flipped[: solution_ref.shape[0], : solution_ref.shape[1]]


def backward_kernel(
    per_share, chunks_ref, scales_ref, live_ref, forward_ref, codes, diag, result_ref, wide, picked
):
    blocks, block_len = diag.shape[0], diag.shape[1]
    rows, rhs_count = codes.shape[0], forward_ref.shape[0]
    half = per_share // 2
    factors = factor_columns(scales_ref, live_ref)
    wide[...] = chunks_ref[...].astype(F32)
    for peer in range(rows // per_share):
        first = peer * per_share
        picked[first : first + per_share, :LANES] = wide[peer, :per_share, :]
        tail = wide[peer, per_share : per_share + half, :]
        picked[first : first + half, LANES:] = tail
        picked[first + half : first + per_share, LANES:] = pltpu.roll(tail, HALF, 1)
    weighted = []
    for group in range(0, rows, LANES):
        span = slice(group, min(group + LANES, rows))
        count = span.stop - span.start
        value = picked[span, :] * factors[:count, group // LANES : group // LANES + 1]
        weighted.append(value.T[:rhs_count].astype(BF16))
    weighted = jnp.concatenate(weighted, axis=1)
    for block in range(blocks):
        columns = slice(block * block_len, (block + 1) * block_len)
        update = dot(weighted, codes[:, columns])
        misfit = (forward_ref[:, columns].astype(F32) - update).astype(BF16)
        result_ref[:, columns] = dot(misfit, diag[block], 1, 1).astype(BF16)


def params(limit):
    return pltpu.CompilerParams(vmem_limit_bytes=limit)


def cost(flops, moved):
    return pl.CostEstimate(flops=flops, bytes_accessed=moved, transcendentals=0)


def on_device(rhs_local, diag_inv, codes, row_scales, sep_index, live_rows, rhs_sep, root_inv):
    rhs_count, local_len = rhs_local.shape
    per_dev, block_len = (diag_inv.shape[0], diag_inv.shape[1])
    coupled_rows = codes.shape[0]
    share_len, sep_len = root_inv.shape
    tile_count = lax.axis_size("tile")
    grid_count = lax.axis_size("grid")
    per_share = coupled_rows // tile_count
    chunk_rows = round_up(per_share + per_share // 2 + 1, 16)
    own_rhs = rhs_count // grid_count
    own_pad = own_rhs * 2 // 3
    assert own_rhs == 12 and share_len == SPLIT and rhs_count == LANES + HALF

    groups = -(-coupled_rows // LANES)
    scales = jnp.pad(row_scales, (0, groups * LANES - coupled_rows)).reshape(groups, LANES)
    indices = jnp.pad(sep_index, (0, groups * LANES - coupled_rows)).reshape(groups, LANES)

    forward_flat, chunks = pl.pallas_call(
        functools.partial(forward_kernel, per_share, share_len),
        out_shape=(
            jax.ShapeDtypeStruct((rhs_count, local_len), BF16),
            jax.ShapeDtypeStruct((tile_count, chunk_rows, LANES), BF16),
        ),
        in_specs=[HBM, HBM, HBM, VMEM, VMEM, SMEM],
        out_specs=(VMEM, VMEM),
        scratch_shapes=[
            pltpu.VMEM((rhs_count, local_len), BF16),
            pltpu.VMEM(diag_inv.shape, BF16),
            pltpu.VMEM(codes.shape, BF16),
            pltpu.VMEM((coupled_rows, 2 * LANES), F32),
            pltpu.VMEM((tile_count, chunk_rows, LANES), F32),
            pltpu.SemaphoreType.DMA((2 + per_dev,)),
        ],
        compiler_params=params(ALL_VMEM),
        cost_estimate=cost(2 * rhs_count * local_len * (block_len + coupled_rows), 5 << 20),
        name="forward",
    )(rhs_local, diag_inv, codes, scales, indices, live_rows)
    arrived = lax.all_to_all(chunks, "tile", 0, 0, tiled=True)
    weight_rows = round_up(3 * share_len, LANES)
    weights = pl.pallas_call(
        weights_kernel,
        out_shape=jax.ShapeDtypeStruct((weight_rows, tile_count * LANES), BF16),
        in_specs=[VMEM],
        out_specs=VMEM,
        compiler_params=params(4 * MIB),
        cost_estimate=cost(share_len * sep_len * 16, 3 << 20),
        name="weights",
    )(root_inv)
    right = lax.dynamic_slice_in_dim(rhs_sep, lax.axis_index("grid") * own_rhs, own_rhs, 0)
    beside = jnp.concatenate([right[own_pad:, : SPLIT // 2], right[own_pad:, SPLIT // 2 :]], axis=0)
    right = jnp.concatenate([right[:own_pad], beside], axis=1).astype(F32)
    right = jnp.pad(right, ((0, 0), (0, LANES - right.shape[1])))
    arrived, weights, right = lax.optimization_barrier((arrived, weights, right))
    onehot, sums = pl.pallas_call(
        functools.partial(sum_kernel, per_share),
        out_shape=(
            jax.ShapeDtypeStruct((tile_count * chunk_rows, 3 * LANES), BF16),
            jax.ShapeDtypeStruct((grid_count, own_pad, LANES), F32),
        ),
        in_specs=[VMEM],
        out_specs=(VMEM, VMEM),
        scratch_shapes=[
            pltpu.VMEM((tile_count, chunk_rows, LANES), F32),
            pltpu.VMEM((LANES, LANES), F32),
            pltpu.VMEM((rhs_count, LANES), F32),
            pltpu.VMEM((rhs_count, LANES), F32),
            pltpu.VMEM((rhs_count, LANES), F32),
        ],
        compiler_params=params(8 * MIB),
        cost_estimate=cost(2 * tile_count * chunk_rows * 3 * LANES * LANES, 1 << 20),
        name="gather_sum",
    )(arrived)
    arrived_sums = lax.all_to_all(sums, "grid", 0, 0, tiled=True)
    root_part = pl.pallas_call(
        root_forward_kernel,
        out_shape=jax.ShapeDtypeStruct((tile_count, own_pad, LANES), BF16),
        in_specs=[VMEM, VMEM, VMEM],
        out_specs=VMEM,
        compiler_params=params(4 * MIB),
        cost_estimate=cost(2 * own_pad * weight_rows * tile_count * LANES, 2 << 20),
        name="root_forward",
    )(arrived_sums, right, weights)
    forward_sep = pl.pallas_call(
        root_middle_kernel,
        out_shape=jax.ShapeDtypeStruct((tile_count, own_pad, LANES), BF16),
        in_specs=[VMEM],
        out_specs=VMEM,
        compiler_params=params(2 * MIB),
        name="root_middle",
    )(lax.all_to_all(root_part, "tile", 0, 0, tiled=True))
    forward_sep = lax.all_to_all(forward_sep, "tile", 0, 0, tiled=True)
    solved = pl.pallas_call(
        root_backward_kernel,
        out_shape=jax.ShapeDtypeStruct((grid_count, own_pad, LANES), BF16),
        in_specs=[VMEM, VMEM],
        out_specs=VMEM,
        compiler_params=params(4 * MIB),
        cost_estimate=cost(2 * own_pad * weight_rows * tile_count * LANES, 2 << 20),
        name="root_backward",
    )(forward_sep, weights)
    solved = lax.all_to_all(solved, "grid", 0, 0, tiled=True)
    solution_sep, picked = pl.pallas_call(
        spread_kernel,
        out_shape=(
            jax.ShapeDtypeStruct((share_len, rhs_count), F32),
            jax.ShapeDtypeStruct((tile_count, chunk_rows, LANES), BF16),
        ),
        in_specs=[VMEM, VMEM],
        out_specs=(VMEM, VMEM),
        scratch_shapes=[
            pltpu.VMEM((3, grid_count * own_pad, LANES), F32),
            pltpu.VMEM((rhs_count, LANES), F32),
            pltpu.VMEM((LANES, 3 * LANES), BF16),
        ],
        compiler_params=params(6 * MIB),
        cost_estimate=cost(2 * tile_count * chunk_rows * 3 * LANES * LANES, 1 << 20),
        name="spread",
    )(solved, onehot)
    picked = lax.all_to_all(picked, "tile", 0, 0, tiled=True)
    result = pl.pallas_call(
        functools.partial(backward_kernel, per_share),
        out_shape=jax.ShapeDtypeStruct((rhs_count, local_len), BF16),
        in_specs=[VMEM, VMEM, SMEM, VMEM, VMEM, VMEM],
        out_specs=VMEM,
        scratch_shapes=[
            pltpu.VMEM((tile_count, chunk_rows, LANES), F32),
            pltpu.VMEM((coupled_rows, 2 * LANES), F32),
        ],
        compiler_params=params(16 * MIB),
        cost_estimate=cost(2 * rhs_count * local_len * (block_len + coupled_rows), 5 << 20),
        name="backward",
    )(picked, scales, live_rows, forward_flat, codes, diag_inv)
    return (result, solution_sep.T)


def solution(mesh):
    return jax.shard_map(
        on_device,
        mesh=mesh,
        in_specs=(
            P(None, ("grid", "tile")),
            P(("grid", "tile"), None, None),
            P(("grid", "tile"), None),
            P(("grid", "tile")),
            P(("grid", "tile")),
            P(("grid", "tile")),
            P(None, "tile"),
            P("tile", None),
        ),
        out_specs=(P(None, ("grid", "tile")), P(None, "tile")),
        check_vma=False,
    )
```

```python
import functools

import jax
import jax.numpy as jnp
from jax import lax
from jax.experimental import pallas as pl
from jax.experimental.pallas import tpu as pltpu
from jax.sharding import PartitionSpec as P

LANES = 128
HALF = 64
SPLIT = 80
F32 = jnp.float32
BF16 = jnp.bfloat16
MIB = 1024 * 1024
ALL_VMEM = 67043328
VMEM = pl.BlockSpec(memory_space=pltpu.VMEM)
SMEM = pl.BlockSpec(memory_space=pltpu.SMEM)
HBM = pl.BlockSpec(memory_space=pltpu.HBM)


def round_up(value, step):
    return -(-value // step) * step


def factor_columns(scales_ref, live_ref):
    groups = scales_ref.shape[0]
    row = lax.broadcasted_iota(jnp.int32, (groups, LANES), 0)
    lane = lax.broadcasted_iota(jnp.int32, (groups, LANES), 1)
    live = (row * LANES + lane) < live_ref[0]
    factors = scales_ref[...] * live.astype(F32)
    if groups < LANES:
        factors = jnp.concatenate([factors, jnp.zeros((LANES - groups, LANES), F32)], axis=0)
    return factors.T


def dot(left, right, left_dim=1, right_dim=0):
    return lax.dot_general(
        left, right, (((left_dim,), (right_dim,)), ((), ())), preferred_element_type=F32
    )


def offset_rows(index_ref, peers, per_share, share_len):
    groups = index_ref.shape[0]
    table = index_ref[...].astype(F32)
    if groups < LANES:
        table = jnp.concatenate([table, jnp.zeros((LANES - groups, LANES), F32)], axis=0)
    table = table.T
    row = lax.broadcasted_iota(jnp.int32, (LANES, LANES), 0).astype(F32)
    lane = lax.broadcasted_iota(jnp.int32, (LANES, LANES), 1).astype(F32)
    peer_row = lax.broadcasted_iota(jnp.int32, (peers, LANES), 0).astype(F32)
    peer_lane = lax.broadcasted_iota(jnp.int32, (peers, LANES), 1).astype(F32)
    total = jnp.zeros((peers, LANES), F32)
    for group in range(groups):
        peer = jnp.floor((row + (group * LANES + 0.5)) * (1.0 / per_share))
        place = row + group * LANES - peer * per_share
        spread = jnp.where(place == lane, table[:, group : group + 1] - peer * share_len, 0.0)
        owner = jnp.floor((peer_lane + (group * LANES + 0.5)) * (1.0 / per_share))
        chosen = (owner == peer_row).astype(F32)
        total = total + dot(chosen.astype(BF16), spread.astype(BF16))
    return total


def forward_kernel(
    per_share, share_len, rhs_hbm, diag_hbm, codes_hbm, scales_ref, index_ref, live_ref,
    forward_hbm, chunks_hbm,
    rhs, diag, codes, coupled, packed, forward_ref, chunks, sems,
):
    blocks, block_len = diag.shape[0], diag.shape[1]
    rows, rhs_count = codes.shape[0], rhs.shape[0]
    half = per_share // 2
    copies = [pltpu.make_async_copy(rhs_hbm, rhs, sems.at[0])]
    for block in range(blocks):
        copies.append(
            pltpu.make_async_copy(diag_hbm.at[block], diag.at[block], sems.at[1 + block])
        )
    copies.append(pltpu.make_async_copy(codes_hbm, codes, sems.at[1 + blocks]))
    for copy in copies:
        copy.start()
    factors = factor_columns(scales_ref, live_ref)
    offsets = offset_rows(index_ref, rows // per_share, per_share, share_len)
    packed[...] = jnp.zeros_like(packed)
    copies[0].wait()
    for block in range(blocks):
        copies[1 + block].wait()
        columns = slice(block * block_len, (block + 1) * block_len)
        forward_ref[:, columns] = dot(rhs[:, columns], diag[block]).astype(BF16)
    copies[-1].wait()
    outgoing = [pltpu.make_async_copy(forward_ref, forward_hbm, sems.at[2 + blocks])]
    outgoing[0].start()
    coupled_sums = dot(codes[...], forward_ref[...], 1, 1)
    for group in range(0, rows, LANES):
        span = slice(group, min(group + LANES, rows))
        count = span.stop - span.start
        value = coupled_sums[span, :] * factors[:count, group // LANES : group // LANES + 1]
        coupled[span, :LANES] = value[:, :LANES]
        tail = value[:, LANES:]
        coupled[span, LANES : LANES + HALF] = tail
        coupled[span, LANES + HALF :] = tail
    low_lane = lax.broadcasted_iota(jnp.int32, (half, LANES), 1) < HALF
    peers = rows // per_share
    for part in range(2):
        span = slice(part * peers // 2, (part + 1) * peers // 2)
        for peer in range(span.start, span.stop):
            first = peer * per_share
            packed[peer, :per_share, :] = coupled[first : first + per_share, :LANES]
            packed[peer, per_share : per_share + half, :] = jnp.where(
                low_lane,
                coupled[first : first + half, LANES:],
                coupled[first + half : first + per_share, LANES:],
            )
            packed[peer, per_share + half : per_share + half + 1, :] = offsets[peer : peer + 1, :]
        chunks[span] = packed[span].astype(BF16)
        copy = pltpu.make_async_copy(
            chunks.at[span], chunks_hbm.at[span], sems.at[3 + blocks + part]
        )
        copy.start()
        outgoing.append(copy)
    for copy in outgoing:
        copy.wait()


def sum_kernel(per_share, chunks_ref, hot_ref, sums_ref, wide, table, total, early, late):
    peers, chunk_rows = chunks_ref.shape[0], chunks_ref.shape[1]
    members, own_pad = sums_ref.shape[0], sums_ref.shape[1]
    half = per_share // 2
    wide[...] = chunks_ref[...].astype(F32)
    for peer in range(peers):
        table[peer : peer + 1, :] = wide[peer, per_share + half : per_share + half + 1, :]
    if peers < LANES:
        table[peers:, :] = jnp.zeros((LANES - peers, LANES), F32)
    offsets = table[...].T
    row = lax.broadcasted_iota(jnp.int32, (LANES, LANES), 0)
    tail_row = jnp.logical_and(row >= per_share, row < per_share + half)
    shifts = (
        jnp.where(row < per_share, offsets, -1.0),
        jnp.where(tail_row, pltpu.roll(offsets, per_share, 0), -1.0),
        jnp.where(tail_row, pltpu.roll(offsets, half, 0), -1.0),
    )
    lane = lax.broadcasted_iota(jnp.int32, (chunk_rows, LANES), 1).astype(F32)
    for peer in range(peers):
        span = slice(peer * chunk_rows, (peer + 1) * chunk_rows)
        for part, shifted in enumerate(shifts):
            hit = shifted[:chunk_rows, peer : peer + 1] == lane
            hot_ref[span, part * LANES : (part + 1) * LANES] = hit.astype(F32).astype(BF16)
    values = wide[...].reshape(peers * chunk_rows, LANES).T.astype(BF16)
    result = dot(values, hot_ref[...])
    total[:LANES, :] = result[:, :LANES]
    total[LANES:, :] = result[:HALF, LANES : 2 * LANES] + result[HALF:, 2 * LANES :]
    value = total[...]
    early[...] = pltpu.roll(value, SPLIT, 1)
    late[...] = pltpu.roll(value, SPLIT // 2, 1)
    quad = own_pad // 2
    lane = lax.broadcasted_iota(jnp.int32, (quad, LANES), 1)
    for member in range(members):
        first = member * 3 * quad
        for part, moved in enumerate((early, late)):
            extra = jnp.where(lane < SPLIT * 3 // 2, moved[first + 2 * quad : first + 3 * quad, :], 0.0)
            begin = first + part * quad
            sums_ref[member, part * quad : (part + 1) * quad, :] = jnp.where(
                lane < SPLIT, total[begin : begin + quad, :], extra
            )


def weights_kernel(root_ref, weights_ref):
    share_len, sep_len = root_ref.shape
    lane = lax.broadcasted_iota(jnp.int32, (share_len, LANES), 1)
    beside = jnp.logical_and(lane >= SPLIT, lane < SPLIT * 3 // 2)
    weights_ref[3 * share_len :, :] = jnp.zeros_like(weights_ref[3 * share_len :, :])
    for peer in range(sep_len // share_len):
        base = peer * share_len // LANES * LANES
        shift = peer * share_len - base
        width = LANES if shift + share_len <= LANES else 2 * LANES
        block = root_ref[:, base : base + width].astype(F32)
        if shift:
            block = pltpu.roll(block, width - shift, 1)
        block = block[:, :LANES]
        columns = slice(peer * LANES, (peer + 1) * LANES)
        plain = jnp.where(lane < SPLIT, block, 0.0)
        first = jnp.where(beside, pltpu.roll(block, SPLIT, 1), 0.0)
        second = jnp.where(beside, pltpu.roll(block, SPLIT // 2, 1), 0.0)
        weights_ref[:share_len, columns] = plain.astype(BF16)
        weights_ref[share_len : 2 * share_len, columns] = first.astype(BF16)
        weights_ref[2 * share_len : 3 * share_len, columns] = second.astype(BF16)


def root_forward_kernel(sums_ref, right_ref, weights_ref, parts_ref):
    gathered = jnp.sum(sums_ref[...], axis=0)
    residue = (right_ref[...] - gathered).astype(BF16).astype(F32)
    row = lax.broadcasted_iota(jnp.int32, residue.shape, 0)
    lane = lax.broadcasted_iota(jnp.int32, residue.shape, 1)
    top = row < 4
    near = pltpu.roll(residue, LANES - SPLIT, 1)
    far = pltpu.roll(residue, LANES - SPLIT // 2, 1)
    upper = jnp.where(lane < SPLIT // 2, near, pltpu.roll(far, 4, 0))
    lower = jnp.where(lane < SPLIT // 2, pltpu.roll(near, 4, 0), far)
    whole = lane < SPLIT
    upper = pltpu.roll(jnp.where(jnp.logical_and(whole, top), upper, 0.0), SPLIT, 1)
    lower = jnp.where(jnp.logical_and(whole, jnp.logical_not(top)), lower, 0.0)
    lower = pltpu.roll(lower, 2 * SPLIT - LANES, 1)
    left = jnp.where(whole, residue, upper)
    right = jnp.where(lane < 2 * SPLIT - LANES, upper, lower)
    operand = jnp.concatenate([left, right], axis=1).astype(BF16)
    result = dot(operand, weights_ref[...]).astype(BF16)
    for peer in range(parts_ref.shape[0]):
        parts_ref[peer] = result[:, peer * LANES : (peer + 1) * LANES]


def root_middle_kernel(parts_ref, forward_ref):
    total = jnp.sum(parts_ref[...].astype(F32), axis=0).astype(BF16)
    forward_ref[...] = jnp.broadcast_to(total[None], forward_ref.shape)


def root_backward_kernel(forward_ref, weights_ref, solved_ref):
    peers = forward_ref.shape[0]
    operand = jnp.concatenate([forward_ref[peer] for peer in range(peers)], axis=1)
    result = dot(operand, weights_ref[...], 1, 1)
    left, right = result[:, :LANES], result[:, LANES:]
    row = lax.broadcasted_iota(jnp.int32, left.shape, 0)
    lane = lax.broadcasted_iota(jnp.int32, left.shape, 1)
    gap = LANES - SPLIT
    first = jnp.where(lane < gap, pltpu.roll(left, gap, 1), pltpu.roll(right, gap, 1))
    second = pltpu.roll(right, LANES - (2 * SPLIT - LANES), 1)
    third = first + pltpu.roll(second, 4, 0)
    beside = jnp.where(
        row < 4, pltpu.roll(third, SPLIT, 1), pltpu.roll(pltpu.roll(third, SPLIT // 2, 1), 4, 0)
    )
    packed = jnp.where(lane < SPLIT, left, jnp.where(lane < SPLIT * 3 // 2, beside, 0.0))
    solved_ref[...] = jnp.broadcast_to(packed.astype(BF16)[None], solved_ref.shape)


def spread_kernel(solved_ref, hot_ref, solution_ref, picked_ref, wide, total, picker):
    members, rows = solved_ref.shape[0], solved_ref.shape[1]
    quad = rows // 2
    plain = solved_ref[...].astype(F32).reshape(members * rows, LANES)
    wide[0] = plain
    wide[1] = pltpu.roll(plain, LANES - SPLIT, 1)
    wide[2] = pltpu.roll(plain, LANES - SPLIT // 2, 1)
    lane = lax.broadcasted_iota(jnp.int32, (quad, LANES), 1)
    for member in range(members):
        first, place = member * rows, member * 3 * quad
        total[place : place + rows, :] = wide[0, first : first + rows, :]
        total[place + rows : place + rows + quad, :] = jnp.where(
            lane < SPLIT // 2,
            wide[1, first : first + quad, :],
            wide[2, first + quad : first + rows, :],
        )
    value = jnp.where(lax.broadcasted_iota(jnp.int32, total.shape, 1) < SPLIT, total[...], 0.0)
    tail = value[LANES:, :].astype(BF16)
    nothing = jnp.zeros((HALF, LANES), BF16)
    picker[:, :LANES] = value[:LANES, :].astype(BF16)
    picker[:HALF, LANES : 2 * LANES] = tail
    picker[HALF:, LANES : 2 * LANES] = nothing
    picker[:HALF, 2 * LANES :] = nothing
    picker[HALF:, 2 * LANES :] = tail
    picked = dot(hot_ref[...], picker[...], 1, 1).astype(BF16)
    picked_ref[...] = picked.reshape(picked_ref.shape)
    padded = jnp.concatenate([value, jnp.zeros((HALF, LANES), F32)], axis=0)
    flipped = padded.T
    solution_ref[...] = flipped[: solution_ref.shape[0], : solution_ref.shape[1]]


def backward_kernel(
    per_share, chunks_ref, scales_ref, live_ref, forward_ref, codes, diag, result_hbm,
    wide, picked, result, sems,
):
    blocks, block_len = diag.shape[0], diag.shape[1]
    rows, rhs_count = codes.shape[0], forward_ref.shape[0]
    half = per_share // 2
    factors = factor_columns(scales_ref, live_ref)
    wide[...] = chunks_ref[...].astype(F32)
    for peer in range(rows // per_share):
        first = peer * per_share
        picked[first : first + per_share, :LANES] = wide[peer, :per_share, :]
        tail = wide[peer, per_share : per_share + half, :]
        picked[first : first + half, LANES:] = tail
        picked[first + half : first + per_share, LANES:] = pltpu.roll(tail, HALF, 1)
    weighted = []
    for group in range(0, rows, LANES):
        span = slice(group, min(group + LANES, rows))
        count = span.stop - span.start
        value = picked[span, :] * factors[:count, group // LANES : group // LANES + 1]
        weighted.append(value.T[:rhs_count].astype(BF16))
    weighted = jnp.concatenate(weighted, axis=1)
    copies = []
    for block in range(blocks):
        columns = slice(block * block_len, (block + 1) * block_len)
        update = dot(weighted, codes[:, columns])
        misfit = (forward_ref[:, columns].astype(F32) - update).astype(BF16)
        result[block] = dot(misfit, diag[block], 1, 1).astype(BF16)
        copy = pltpu.make_async_copy(result.at[block], result_hbm.at[:, columns], sems.at[block])
        copy.start()
        copies.append(copy)
    for copy in copies:
        copy.wait()


def params(limit):
    return pltpu.CompilerParams(vmem_limit_bytes=limit)


def cost(flops, moved):
    return pl.CostEstimate(flops=flops, bytes_accessed=moved, transcendentals=0)


def on_device(rhs_local, diag_inv, codes, row_scales, sep_index, live_rows, rhs_sep, root_inv):
    rhs_count, local_len = rhs_local.shape
    per_dev, block_len = (diag_inv.shape[0], diag_inv.shape[1])
    coupled_rows = codes.shape[0]
    share_len, sep_len = root_inv.shape
    tile_count = lax.axis_size("tile")
    grid_count = lax.axis_size("grid")
    per_share = coupled_rows // tile_count
    chunk_rows = round_up(per_share + per_share // 2 + 1, 16)
    own_rhs = rhs_count // grid_count
    own_pad = own_rhs * 2 // 3
    assert own_rhs == 12 and share_len == SPLIT and rhs_count == LANES + HALF

    groups = -(-coupled_rows // LANES)
    scales = jnp.pad(row_scales, (0, groups * LANES - coupled_rows)).reshape(groups, LANES)
    indices = jnp.pad(sep_index, (0, groups * LANES - coupled_rows)).reshape(groups, LANES)

    forward_flat, chunks = pl.pallas_call(
        functools.partial(forward_kernel, per_share, share_len),
        out_shape=(
            jax.ShapeDtypeStruct((rhs_count, local_len), BF16),
            jax.ShapeDtypeStruct((tile_count, chunk_rows, LANES), BF16),
        ),
        in_specs=[HBM, HBM, HBM, VMEM, VMEM, SMEM],
        out_specs=(HBM, HBM),
        scratch_shapes=[
            pltpu.VMEM((rhs_count, local_len), BF16),
            pltpu.VMEM(diag_inv.shape, BF16),
            pltpu.VMEM(codes.shape, BF16),
            pltpu.VMEM((coupled_rows, 2 * LANES), F32),
            pltpu.VMEM((tile_count, chunk_rows, LANES), F32),
            pltpu.VMEM((rhs_count, local_len), BF16),
            pltpu.VMEM((tile_count, chunk_rows, LANES), BF16),
            pltpu.SemaphoreType.DMA((5 + per_dev,)),
        ],
        compiler_params=params(ALL_VMEM),
        cost_estimate=cost(2 * rhs_count * local_len * (block_len + coupled_rows), 5 << 20),
        name="forward",
    )(rhs_local, diag_inv, codes, scales, indices, live_rows)
    arrived = lax.all_to_all(chunks, "tile", 0, 0, tiled=True)
    weight_rows = round_up(3 * share_len, LANES)
    weights = pl.pallas_call(
        weights_kernel,
        out_shape=jax.ShapeDtypeStruct((weight_rows, tile_count * LANES), BF16),
        in_specs=[VMEM],
        out_specs=VMEM,
        compiler_params=params(4 * MIB),
        cost_estimate=cost(share_len * sep_len * 16, 3 << 20),
        name="weights",
    )(root_inv)
    right = lax.dynamic_slice_in_dim(rhs_sep, lax.axis_index("grid") * own_rhs, own_rhs, 0)
    beside = jnp.concatenate([right[own_pad:, : SPLIT // 2], right[own_pad:, SPLIT // 2 :]], axis=0)
    right = jnp.concatenate([right[:own_pad], beside], axis=1).astype(F32)
    right = jnp.pad(right, ((0, 0), (0, LANES - right.shape[1])))
    arrived, weights, right = lax.optimization_barrier((arrived, weights, right))
    onehot, sums = pl.pallas_call(
        functools.partial(sum_kernel, per_share),
        out_shape=(
            jax.ShapeDtypeStruct((tile_count * chunk_rows, 3 * LANES), BF16),
            jax.ShapeDtypeStruct((grid_count, own_pad, LANES), F32),
        ),
        in_specs=[VMEM],
        out_specs=(VMEM, VMEM),
        scratch_shapes=[
            pltpu.VMEM((tile_count, chunk_rows, LANES), F32),
            pltpu.VMEM((LANES, LANES), F32),
            pltpu.VMEM((rhs_count, LANES), F32),
            pltpu.VMEM((rhs_count, LANES), F32),
            pltpu.VMEM((rhs_count, LANES), F32),
        ],
        compiler_params=params(8 * MIB),
        cost_estimate=cost(2 * tile_count * chunk_rows * 3 * LANES * LANES, 1 << 20),
        name="gather_sum",
    )(arrived)
    arrived_sums = lax.all_to_all(sums, "grid", 0, 0, tiled=True)
    root_part = pl.pallas_call(
        root_forward_kernel,
        out_shape=jax.ShapeDtypeStruct((tile_count, own_pad, LANES), BF16),
        in_specs=[VMEM, VMEM, VMEM],
        out_specs=VMEM,
        compiler_params=params(4 * MIB),
        cost_estimate=cost(2 * own_pad * weight_rows * tile_count * LANES, 2 << 20),
        name="root_forward",
    )(arrived_sums, right, weights)
    forward_sep = pl.pallas_call(
        root_middle_kernel,
        out_shape=jax.ShapeDtypeStruct((tile_count, own_pad, LANES), BF16),
        in_specs=[VMEM],
        out_specs=VMEM,
        compiler_params=params(2 * MIB),
        name="root_middle",
    )(lax.all_to_all(root_part, "tile", 0, 0, tiled=True))
    forward_sep = lax.all_to_all(forward_sep, "tile", 0, 0, tiled=True)
    solved = pl.pallas_call(
        root_backward_kernel,
        out_shape=jax.ShapeDtypeStruct((grid_count, own_pad, LANES), BF16),
        in_specs=[VMEM, VMEM],
        out_specs=VMEM,
        compiler_params=params(4 * MIB),
        cost_estimate=cost(2 * own_pad * weight_rows * tile_count * LANES, 2 << 20),
        name="root_backward",
    )(forward_sep, weights)
    solved = lax.all_to_all(solved, "grid", 0, 0, tiled=True)
    solution_sep, picked = pl.pallas_call(
        spread_kernel,
        out_shape=(
            jax.ShapeDtypeStruct((share_len, rhs_count), F32),
            jax.ShapeDtypeStruct((tile_count, chunk_rows, LANES), BF16),
        ),
        in_specs=[VMEM, VMEM],
        out_specs=(VMEM, VMEM),
        scratch_shapes=[
            pltpu.VMEM((3, grid_count * own_pad, LANES), F32),
            pltpu.VMEM((rhs_count, LANES), F32),
            pltpu.VMEM((LANES, 3 * LANES), BF16),
        ],
        compiler_params=params(6 * MIB),
        cost_estimate=cost(2 * tile_count * chunk_rows * 3 * LANES * LANES, 1 << 20),
        name="spread",
    )(solved, onehot)
    picked = lax.all_to_all(picked, "tile", 0, 0, tiled=True)
    result = pl.pallas_call(
        functools.partial(backward_kernel, per_share),
        out_shape=jax.ShapeDtypeStruct((rhs_count, local_len), BF16),
        in_specs=[VMEM, VMEM, SMEM, VMEM, VMEM, VMEM],
        out_specs=HBM,
        scratch_shapes=[
            pltpu.VMEM((tile_count, chunk_rows, LANES), F32),
            pltpu.VMEM((coupled_rows, 2 * LANES), F32),
            pltpu.VMEM((per_dev, rhs_count, block_len), BF16),
            pltpu.SemaphoreType.DMA((per_dev,)),
        ],
        compiler_params=params(16 * MIB),
        cost_estimate=cost(2 * rhs_count * local_len * (block_len + coupled_rows), 5 << 20),
        name="backward",
    )(picked, scales, live_rows, forward_flat, codes, diag_inv)
    return (result, solution_sep.T)


def solution(mesh):
    return jax.shard_map(
        on_device,
        mesh=mesh,
        in_specs=(
            P(None, ("grid", "tile")),
            P(("grid", "tile"), None, None),
            P(("grid", "tile"), None),
            P(("grid", "tile")),
            P(("grid", "tile")),
            P(("grid", "tile")),
            P(None, "tile"),
            P("tile", None),
        ),
        out_specs=(P(None, ("grid", "tile")), P(None, "tile")),
        check_vma=False,
    )
```

```python
import functools

import jax
import jax.numpy as jnp
from jax import lax
from jax.experimental import pallas as pl
from jax.experimental.pallas import tpu as pltpu
from jax.sharding import PartitionSpec as P

LANES = 128
HALF = 64
SPLIT = 80
F32 = jnp.float32
BF16 = jnp.bfloat16
MIB = 1024 * 1024
ALL_VMEM = 67043328
VMEM = pl.BlockSpec(memory_space=pltpu.VMEM)
SMEM = pl.BlockSpec(memory_space=pltpu.SMEM)
HBM = pl.BlockSpec(memory_space=pltpu.HBM)


def round_up(value, step):
    return -(-value // step) * step


def factor_columns(scales_ref, live_ref):
    groups = scales_ref.shape[0]
    row = lax.broadcasted_iota(jnp.int32, (groups, LANES), 0)
    lane = lax.broadcasted_iota(jnp.int32, (groups, LANES), 1)
    live = (row * LANES + lane) < live_ref[0]
    factors = scales_ref[...] * live.astype(F32)
    if groups < LANES:
        factors = jnp.concatenate([factors, jnp.zeros((LANES - groups, LANES), F32)], axis=0)
    return factors.T


def dot(left, right, left_dim=1, right_dim=0):
    return lax.dot_general(
        left, right, (((left_dim,), (right_dim,)), ((), ())), preferred_element_type=F32
    )


def offset_rows(index_ref, peers, per_share, share_len):
    groups = index_ref.shape[0]
    table = index_ref[...].astype(F32)
    if groups < LANES:
        table = jnp.concatenate([table, jnp.zeros((LANES - groups, LANES), F32)], axis=0)
    table = table.T
    row = lax.broadcasted_iota(jnp.int32, (LANES, LANES), 0).astype(F32)
    lane = lax.broadcasted_iota(jnp.int32, (LANES, LANES), 1).astype(F32)
    peer_row = lax.broadcasted_iota(jnp.int32, (peers, LANES), 0).astype(F32)
    peer_lane = lax.broadcasted_iota(jnp.int32, (peers, LANES), 1).astype(F32)
    total = jnp.zeros((peers, LANES), F32)
    for group in range(groups):
        peer = jnp.floor((row + (group * LANES + 0.5)) * (1.0 / per_share))
        place = row + group * LANES - peer * per_share
        spread = jnp.where(place == lane, table[:, group : group + 1] - peer * share_len, 0.0)
        owner = jnp.floor((peer_lane + (group * LANES + 0.5)) * (1.0 / per_share))
        chosen = (owner == peer_row).astype(F32)
        total = total + dot(chosen.astype(BF16), spread.astype(BF16))
    return total


def forward_kernel(
    per_share, share_len, rhs_hbm, diag_hbm, codes_hbm, scales_ref, index_ref, live_ref,
    forward_hbm, chunks_hbm,
    rhs, diag, codes, coupled, packed, forward_ref, chunks, sems,
):
    blocks, block_len = diag.shape[0], diag.shape[1]
    rows, rhs_count = codes.shape[0], rhs.shape[0]
    half = per_share // 2
    copies = [pltpu.make_async_copy(rhs_hbm, rhs, sems.at[0])]
    for block in range(blocks):
        copies.append(
            pltpu.make_async_copy(diag_hbm.at[block], diag.at[block], sems.at[1 + block])
        )
    copies.append(pltpu.make_async_copy(codes_hbm, codes, sems.at[1 + blocks]))
    for copy in copies:
        copy.start()
    factors = factor_columns(scales_ref, live_ref)
    offsets = offset_rows(index_ref, rows // per_share, per_share, share_len)
    packed[...] = jnp.zeros_like(packed)
    copies[0].wait()
    for block in range(blocks):
        copies[1 + block].wait()
        columns = slice(block * block_len, (block + 1) * block_len)
        forward_ref[:, columns] = dot(rhs[:, columns], diag[block]).astype(BF16)
    copies[-1].wait()
    outgoing = [pltpu.make_async_copy(forward_ref, forward_hbm, sems.at[2 + blocks])]
    outgoing[0].start()
    coupled_sums = dot(codes[...], forward_ref[...], 1, 1)
    for group in range(0, rows, LANES):
        span = slice(group, min(group + LANES, rows))
        count = span.stop - span.start
        value = coupled_sums[span, :] * factors[:count, group // LANES : group // LANES + 1]
        coupled[span, :LANES] = value[:, :LANES]
        tail = value[:, LANES:]
        coupled[span, LANES : LANES + HALF] = tail
        coupled[span, LANES + HALF :] = tail
    low_lane = lax.broadcasted_iota(jnp.int32, (half, LANES), 1) < HALF
    peers = rows // per_share
    for part in range(2):
        span = slice(part * peers // 2, (part + 1) * peers // 2)
        for peer in range(span.start, span.stop):
            first = peer * per_share
            packed[peer, :per_share, :] = coupled[first : first + per_share, :LANES]
            packed[peer, per_share : per_share + half, :] = jnp.where(
                low_lane,
                coupled[first : first + half, LANES:],
                coupled[first + half : first + per_share, LANES:],
            )
            packed[peer, per_share + half : per_share + half + 1, :] = offsets[peer : peer + 1, :]
        chunks[span] = packed[span].astype(BF16)
        copy = pltpu.make_async_copy(
            chunks.at[span], chunks_hbm.at[span], sems.at[3 + blocks + part]
        )
        copy.start()
        outgoing.append(copy)
    for copy in outgoing:
        copy.wait()


def sum_kernel(per_share, chunks_ref, hot_ref, sums_ref, wide, table, total, early, late):
    peers, chunk_rows = chunks_ref.shape[0], chunks_ref.shape[1]
    members, own_pad = sums_ref.shape[0], sums_ref.shape[1]
    half = per_share // 2
    wide[...] = chunks_ref[...].astype(F32)
    for peer in range(peers):
        table[peer : peer + 1, :] = wide[peer, per_share + half : per_share + half + 1, :]
    if peers < LANES:
        table[peers:, :] = jnp.zeros((LANES - peers, LANES), F32)
    offsets = table[...].T
    row = lax.broadcasted_iota(jnp.int32, (LANES, LANES), 0)
    tail_row = jnp.logical_and(row >= per_share, row < per_share + half)
    shifts = (
        jnp.where(row < per_share, offsets, -1.0),
        jnp.where(tail_row, pltpu.roll(offsets, per_share, 0), -1.0),
        jnp.where(tail_row, pltpu.roll(offsets, half, 0), -1.0),
    )
    lane = lax.broadcasted_iota(jnp.int32, (chunk_rows, LANES), 1).astype(F32)
    for peer in range(peers):
        span = slice(peer * chunk_rows, (peer + 1) * chunk_rows)
        for part, shifted in enumerate(shifts):
            hit = shifted[:chunk_rows, peer : peer + 1] == lane
            hot_ref[span, part * LANES : (part + 1) * LANES] = hit.astype(F32).astype(BF16)
    values = wide[...].reshape(peers * chunk_rows, LANES).T.astype(BF16)
    result = dot(values, hot_ref[...])
    total[:LANES, :] = result[:, :LANES]
    total[LANES:, :] = result[:HALF, LANES : 2 * LANES] + result[HALF:, 2 * LANES :]
    value = total[...]
    early[...] = pltpu.roll(value, SPLIT, 1)
    late[...] = pltpu.roll(value, SPLIT // 2, 1)
    quad = own_pad // 2
    lane = lax.broadcasted_iota(jnp.int32, (quad, LANES), 1)
    for member in range(members):
        first = member * 3 * quad
        for part, moved in enumerate((early, late)):
            extra = jnp.where(lane < SPLIT * 3 // 2, moved[first + 2 * quad : first + 3 * quad, :], 0.0)
            begin = first + part * quad
            sums_ref[member, part * quad : (part + 1) * quad, :] = jnp.where(
                lane < SPLIT, total[begin : begin + quad, :], extra
            )


def weights_kernel(root_ref, weights_ref):
    share_len, sep_len = root_ref.shape
    lane = lax.broadcasted_iota(jnp.int32, (share_len, LANES), 1)
    beside = jnp.logical_and(lane >= SPLIT, lane < SPLIT * 3 // 2)
    weights_ref[3 * share_len :, :] = jnp.zeros_like(weights_ref[3 * share_len :, :])
    for peer in range(sep_len // share_len):
        base = peer * share_len // LANES * LANES
        shift = peer * share_len - base
        width = LANES if shift + share_len <= LANES else 2 * LANES
        block = root_ref[:, base : base + width].astype(F32)
        if shift:
            block = pltpu.roll(block, width - shift, 1)
        block = block[:, :LANES]
        columns = slice(peer * LANES, (peer + 1) * LANES)
        plain = jnp.where(lane < SPLIT, block, 0.0)
        first = jnp.where(beside, pltpu.roll(block, SPLIT, 1), 0.0)
        second = jnp.where(beside, pltpu.roll(block, SPLIT // 2, 1), 0.0)
        weights_ref[:share_len, columns] = plain.astype(BF16)
        weights_ref[share_len : 2 * share_len, columns] = first.astype(BF16)
        weights_ref[2 * share_len : 3 * share_len, columns] = second.astype(BF16)


def root_forward_kernel(sums_ref, right_ref, weights_ref, parts_ref):
    gathered = jnp.sum(sums_ref[...], axis=0)
    residue = (right_ref[...] - gathered).astype(BF16).astype(F32)
    row = lax.broadcasted_iota(jnp.int32, residue.shape, 0)
    lane = lax.broadcasted_iota(jnp.int32, residue.shape, 1)
    top = row < 4
    near = pltpu.roll(residue, LANES - SPLIT, 1)
    far = pltpu.roll(residue, LANES - SPLIT // 2, 1)
    upper = jnp.where(lane < SPLIT // 2, near, pltpu.roll(far, 4, 0))
    lower = jnp.where(lane < SPLIT // 2, pltpu.roll(near, 4, 0), far)
    whole = lane < SPLIT
    upper = pltpu.roll(jnp.where(jnp.logical_and(whole, top), upper, 0.0), SPLIT, 1)
    lower = jnp.where(jnp.logical_and(whole, jnp.logical_not(top)), lower, 0.0)
    lower = pltpu.roll(lower, 2 * SPLIT - LANES, 1)
    left = jnp.where(whole, residue, upper)
    right = jnp.where(lane < 2 * SPLIT - LANES, upper, lower)
    operand = jnp.concatenate([left, right], axis=1).astype(BF16)
    result = dot(operand, weights_ref[...]).astype(BF16)
    for peer in range(parts_ref.shape[0]):
        parts_ref[peer] = result[:, peer * LANES : (peer + 1) * LANES]


def root_middle_kernel(parts_ref, forward_ref):
    total = jnp.sum(parts_ref[...].astype(F32), axis=0).astype(BF16)
    forward_ref[...] = jnp.broadcast_to(total[None], forward_ref.shape)


def root_backward_kernel(forward_ref, weights_ref, solved_ref):
    peers = forward_ref.shape[0]
    operand = jnp.concatenate([forward_ref[peer] for peer in range(peers)], axis=1)
    result = dot(operand, weights_ref[...], 1, 1)
    left, right = result[:, :LANES], result[:, LANES:]
    row = lax.broadcasted_iota(jnp.int32, left.shape, 0)
    lane = lax.broadcasted_iota(jnp.int32, left.shape, 1)
    gap = LANES - SPLIT
    first = jnp.where(lane < gap, pltpu.roll(left, gap, 1), pltpu.roll(right, gap, 1))
    second = pltpu.roll(right, LANES - (2 * SPLIT - LANES), 1)
    third = first + pltpu.roll(second, 4, 0)
    beside = jnp.where(
        row < 4, pltpu.roll(third, SPLIT, 1), pltpu.roll(pltpu.roll(third, SPLIT // 2, 1), 4, 0)
    )
    packed = jnp.where(lane < SPLIT, left, jnp.where(lane < SPLIT * 3 // 2, beside, 0.0))
    solved_ref[...] = jnp.broadcast_to(packed.astype(BF16)[None], solved_ref.shape)


def unpack(solved_ref, wide, total):
    members, rows = solved_ref.shape[0], solved_ref.shape[1]
    quad = rows // 2
    plain = solved_ref[...].astype(F32).reshape(members * rows, LANES)
    wide[0] = plain
    wide[1] = pltpu.roll(plain, LANES - SPLIT, 1)
    wide[2] = pltpu.roll(plain, LANES - SPLIT // 2, 1)
    lane = lax.broadcasted_iota(jnp.int32, (quad, LANES), 1)
    for member in range(members):
        first, place = member * rows, member * 3 * quad
        total[place : place + rows, :] = wide[0, first : first + rows, :]
        total[place + rows : place + rows + quad, :] = jnp.where(
            lane < SPLIT // 2,
            wide[1, first : first + quad, :],
            wide[2, first + quad : first + rows, :],
        )
    return jnp.where(lax.broadcasted_iota(jnp.int32, total.shape, 1) < SPLIT, total[...], 0.0)


def spread_kernel(solved_ref, hot_ref, picked_ref, wide, total, picker):
    value = unpack(solved_ref, wide, total)
    tail = value[LANES:, :].astype(BF16)
    nothing = jnp.zeros((HALF, LANES), BF16)
    picker[:, :LANES] = value[:LANES, :].astype(BF16)
    picker[:HALF, LANES : 2 * LANES] = tail
    picker[HALF:, LANES : 2 * LANES] = nothing
    picker[:HALF, 2 * LANES :] = nothing
    picker[HALF:, 2 * LANES :] = tail
    picked = dot(hot_ref[...], picker[...], 1, 1).astype(BF16)
    picked_ref[...] = picked.reshape(picked_ref.shape)


def backward_kernel(
    per_share, chunks_ref, scales_ref, live_ref, forward_ref, codes, diag, solved_ref,
    result_hbm, solution_hbm,
    wide, picked, result, solved_wide, total, solution_rows, sems,
):
    blocks, block_len = diag.shape[0], diag.shape[1]
    value = unpack(solved_ref, solved_wide, total)
    padded = jnp.concatenate([value, jnp.zeros((HALF, LANES), F32)], axis=0)
    flipped = padded.T
    solution_rows[...] = flipped[: solution_rows.shape[0], : solution_rows.shape[1]]
    copies = [pltpu.make_async_copy(solution_rows, solution_hbm, sems.at[blocks])]
    copies[0].start()
    rows, rhs_count = codes.shape[0], forward_ref.shape[0]
    half = per_share // 2
    factors = factor_columns(scales_ref, live_ref)
    wide[...] = chunks_ref[...].astype(F32)
    for peer in range(rows // per_share):
        first = peer * per_share
        picked[first : first + per_share, :LANES] = wide[peer, :per_share, :]
        tail = wide[peer, per_share : per_share + half, :]
        picked[first : first + half, LANES:] = tail
        picked[first + half : first + per_share, LANES:] = pltpu.roll(tail, HALF, 1)
    weighted = []
    for group in range(0, rows, LANES):
        span = slice(group, min(group + LANES, rows))
        count = span.stop - span.start
        value = picked[span, :] * factors[:count, group // LANES : group // LANES + 1]
        weighted.append(value.T[:rhs_count].astype(BF16))
    weighted = jnp.concatenate(weighted, axis=1)
    for block in range(blocks):
        columns = slice(block * block_len, (block + 1) * block_len)
        update = dot(weighted, codes[:, columns])
        misfit = (forward_ref[:, columns].astype(F32) - update).astype(BF16)
        result[block] = dot(misfit, diag[block], 1, 1).astype(BF16)
        copy = pltpu.make_async_copy(result.at[block], result_hbm.at[:, columns], sems.at[block])
        copy.start()
        copies.append(copy)
    for copy in copies:
        copy.wait()


def params(limit):
    return pltpu.CompilerParams(vmem_limit_bytes=limit)


def cost(flops, moved):
    return pl.CostEstimate(flops=flops, bytes_accessed=moved, transcendentals=0)


def on_device(rhs_local, diag_inv, codes, row_scales, sep_index, live_rows, rhs_sep, root_inv):
    rhs_count, local_len = rhs_local.shape
    per_dev, block_len = (diag_inv.shape[0], diag_inv.shape[1])
    coupled_rows = codes.shape[0]
    share_len, sep_len = root_inv.shape
    tile_count = lax.axis_size("tile")
    grid_count = lax.axis_size("grid")
    per_share = coupled_rows // tile_count
    chunk_rows = round_up(per_share + per_share // 2 + 1, 16)
    own_rhs = rhs_count // grid_count
    own_pad = own_rhs * 2 // 3
    assert own_rhs == 12 and share_len == SPLIT and rhs_count == LANES + HALF

    groups = -(-coupled_rows // LANES)
    scales = jnp.pad(row_scales, (0, groups * LANES - coupled_rows)).reshape(groups, LANES)
    indices = jnp.pad(sep_index, (0, groups * LANES - coupled_rows)).reshape(groups, LANES)

    forward_flat, chunks = pl.pallas_call(
        functools.partial(forward_kernel, per_share, share_len),
        out_shape=(
            jax.ShapeDtypeStruct((rhs_count, local_len), BF16),
            jax.ShapeDtypeStruct((tile_count, chunk_rows, LANES), BF16),
        ),
        in_specs=[HBM, HBM, HBM, VMEM, VMEM, SMEM],
        out_specs=(HBM, HBM),
        scratch_shapes=[
            pltpu.VMEM((rhs_count, local_len), BF16),
            pltpu.VMEM(diag_inv.shape, BF16),
            pltpu.VMEM(codes.shape, BF16),
            pltpu.VMEM((coupled_rows, 2 * LANES), F32),
            pltpu.VMEM((tile_count, chunk_rows, LANES), F32),
            pltpu.VMEM((rhs_count, local_len), BF16),
            pltpu.VMEM((tile_count, chunk_rows, LANES), BF16),
            pltpu.SemaphoreType.DMA((5 + per_dev,)),
        ],
        compiler_params=params(ALL_VMEM),
        cost_estimate=cost(2 * rhs_count * local_len * (block_len + coupled_rows), 5 << 20),
        name="forward",
    )(rhs_local, diag_inv, codes, scales, indices, live_rows)
    arrived = lax.all_to_all(chunks, "tile", 0, 0, tiled=True)
    weight_rows = round_up(3 * share_len, LANES)
    weights = pl.pallas_call(
        weights_kernel,
        out_shape=jax.ShapeDtypeStruct((weight_rows, tile_count * LANES), BF16),
        in_specs=[VMEM],
        out_specs=VMEM,
        compiler_params=params(4 * MIB),
        cost_estimate=cost(share_len * sep_len * 16, 3 << 20),
        name="weights",
    )(root_inv)
    right = lax.dynamic_slice_in_dim(rhs_sep, lax.axis_index("grid") * own_rhs, own_rhs, 0)
    beside = jnp.concatenate([right[own_pad:, : SPLIT // 2], right[own_pad:, SPLIT // 2 :]], axis=0)
    right = jnp.concatenate([right[:own_pad], beside], axis=1).astype(F32)
    right = jnp.pad(right, ((0, 0), (0, LANES - right.shape[1])))
    arrived, weights, right = lax.optimization_barrier((arrived, weights, right))
    onehot, sums = pl.pallas_call(
        functools.partial(sum_kernel, per_share),
        out_shape=(
            jax.ShapeDtypeStruct((tile_count * chunk_rows, 3 * LANES), BF16),
            jax.ShapeDtypeStruct((grid_count, own_pad, LANES), F32),
        ),
        in_specs=[VMEM],
        out_specs=(VMEM, VMEM),
        scratch_shapes=[
            pltpu.VMEM((tile_count, chunk_rows, LANES), F32),
            pltpu.VMEM((LANES, LANES), F32),
            pltpu.VMEM((rhs_count, LANES), F32),
            pltpu.VMEM((rhs_count, LANES), F32),
            pltpu.VMEM((rhs_count, LANES), F32),
        ],
        compiler_params=params(8 * MIB),
        cost_estimate=cost(2 * tile_count * chunk_rows * 3 * LANES * LANES, 1 << 20),
        name="gather_sum",
    )(arrived)
    arrived_sums = lax.all_to_all(sums, "grid", 0, 0, tiled=True)
    root_part = pl.pallas_call(
        root_forward_kernel,
        out_shape=jax.ShapeDtypeStruct((tile_count, own_pad, LANES), BF16),
        in_specs=[VMEM, VMEM, VMEM],
        out_specs=VMEM,
        compiler_params=params(4 * MIB),
        cost_estimate=cost(2 * own_pad * weight_rows * tile_count * LANES, 2 << 20),
        name="root_forward",
    )(arrived_sums, right, weights)
    forward_sep = pl.pallas_call(
        root_middle_kernel,
        out_shape=jax.ShapeDtypeStruct((tile_count, own_pad, LANES), BF16),
        in_specs=[VMEM],
        out_specs=VMEM,
        compiler_params=params(2 * MIB),
        name="root_middle",
    )(lax.all_to_all(root_part, "tile", 0, 0, tiled=True))
    forward_sep = lax.all_to_all(forward_sep, "tile", 0, 0, tiled=True)
    solved = pl.pallas_call(
        root_backward_kernel,
        out_shape=jax.ShapeDtypeStruct((grid_count, own_pad, LANES), BF16),
        in_specs=[VMEM, VMEM],
        out_specs=VMEM,
        compiler_params=params(4 * MIB),
        cost_estimate=cost(2 * own_pad * weight_rows * tile_count * LANES, 2 << 20),
        name="root_backward",
    )(forward_sep, weights)
    solved = lax.all_to_all(solved, "grid", 0, 0, tiled=True)
    picked = pl.pallas_call(
        spread_kernel,
        out_shape=jax.ShapeDtypeStruct((tile_count, chunk_rows, LANES), BF16),
        in_specs=[VMEM, VMEM],
        out_specs=VMEM,
        scratch_shapes=[
            pltpu.VMEM((3, grid_count * own_pad, LANES), F32),
            pltpu.VMEM((rhs_count, LANES), F32),
            pltpu.VMEM((LANES, 3 * LANES), BF16),
        ],
        compiler_params=params(6 * MIB),
        cost_estimate=cost(2 * tile_count * chunk_rows * 3 * LANES * LANES, 1 << 20),
        name="spread",
    )(solved, onehot)
    picked = lax.all_to_all(picked, "tile", 0, 0, tiled=True)
    result, solution_sep = pl.pallas_call(
        functools.partial(backward_kernel, per_share),
        out_shape=(
            jax.ShapeDtypeStruct((rhs_count, local_len), BF16),
            jax.ShapeDtypeStruct((share_len, rhs_count), F32),
        ),
        in_specs=[VMEM, VMEM, SMEM, VMEM, VMEM, VMEM, VMEM],
        out_specs=(HBM, HBM),
        scratch_shapes=[
            pltpu.VMEM((tile_count, chunk_rows, LANES), F32),
            pltpu.VMEM((coupled_rows, 2 * LANES), F32),
            pltpu.VMEM((per_dev, rhs_count, block_len), BF16),
            pltpu.VMEM((3, grid_count * own_pad, LANES), F32),
            pltpu.VMEM((rhs_count, LANES), F32),
            pltpu.VMEM((share_len, rhs_count), F32),
            pltpu.SemaphoreType.DMA((per_dev + 1,)),
        ],
        compiler_params=params(16 * MIB),
        cost_estimate=cost(2 * rhs_count * local_len * (block_len + coupled_rows), 5 << 20),
        name="backward",
    )(picked, scales, live_rows, forward_flat, codes, diag_inv, solved)
    return (result, solution_sep.T)


def solution(mesh):
    return jax.shard_map(
        on_device,
        mesh=mesh,
        in_specs=(
            P(None, ("grid", "tile")),
            P(("grid", "tile"), None, None),
            P(("grid", "tile"), None),
            P(("grid", "tile")),
            P(("grid", "tile")),
            P(("grid", "tile")),
            P(None, "tile"),
            P("tile", None),
        ),
        out_specs=(P(None, ("grid", "tile")), P(None, "tile")),
        check_vma=False,
    )
```
